128 devices in a mesh: grp: 4 (over x), dev: 32 (over y, z, core).
Axes of the slice: x: 4, y: 4, z: 4, core: 2. Of those that a mesh axis runs over, the one named last changes fastest.
Arguments:
- locations: float32 [128, 3, 256], P(('grp', 'dev')), may hold values from 0 to 1
- neighbours: int32 [128, 4], P(('grp', 'dev')), may hold values from -1 to 126, as said below
- observations: float32 [128, 8, 256], P(('grp', 'dev')), may hold values from -63 to 63
- noise_prec: float32 [128, 8, 256], P(('grp', 'dev')), may hold values from 0.5 to 4
Outputs:
- solution: float32 [128, 8, 256], P(('grp', 'dev'))
- residual: float32 [128, 8, 256], P(('grp', 'dev'))
The draws below stay inside these ranges and needn't reach their ends.
Inputs may be any that keep to these rules, and one draw needn't show every extreme that they name: `neighbours`: row b holds b - 1 in slot 0 (-1 for block 0); in slot 1 a block drawn from the range from max(b - 1, 0) * 1 to b - 2, or -1 where that range is empty; in slots 2 and 3 two different blocks below min(32, max(b - 1, 0)), -1 in a slot where fewer exist. All listed blocks of a row differ.
All inputs are finite; a program needn't handle non-finite values.
Results may differ from the reference program's by a relative error of at most 0.0003.
Values sent between devices are 32-bit elements; how exact they have to be, the bound alone decides.
A program may use at most 128 MiB of HBM per device.

```python
import math
import jax
import jax.numpy as jnp
from jax import lax

BS = 256
NEIGH = 4
BLK_DEV = 1
NV = 8
ITERS = 2
NBLK = 128
NCOARSE = 32


def draw_neighbours(key, part):
    block_index = jnp.arange(NBLK, dtype=jnp.int32)
    device_index = block_index // BLK_DEV
    window_first = jnp.maximum(device_index - 1, 0) * BLK_DEV
    window_size = jnp.maximum(block_index - 1 - window_first, 0)
    subkeys = jax.random.split(jax.random.fold_in(key, 11), 3)
    near_pick = window_first + jax.random.randint(subkeys[0], (NBLK,), 0, jnp.maximum(window_size, 1))
    near_pick = jnp.where(window_size > 0, near_pick, -1)
    coarse_limit = jnp.minimum(NCOARSE, window_first)
    first_top = coarse_limit - 2
    first_draw = jax.random.randint(subkeys[1], (NBLK,), 0, jnp.maximum(first_top + 1, 1))
    coarse_one = jnp.where(first_top >= 0, first_draw, -1)
    second_top = coarse_limit - 1
    second_draw = jax.random.randint(subkeys[2], (NBLK,), 0, jnp.maximum(second_top + 1, 1))
    second_draw = jnp.where(second_draw == coarse_one, second_top, second_draw)
    coarse_two = jnp.where(second_top >= 0, second_draw, -1)
    return jnp.stack([block_index - 1, near_pick, coarse_one, coarse_two], axis=1).astype(jnp.int32)


def draw_observations(key, part):
    subkeys = jax.random.split(jax.random.fold_in(key, 23), 2)
    values = jnp.clip(jax.random.normal(subkeys[0], (NBLK, NV, BS), jnp.float32), -4.0, 4.0)
    rising = 1.0 + 2.0 * jnp.arange(NBLK, dtype=jnp.float32) / (NBLK - 1)
    field_scale = jnp.exp(jax.random.uniform(subkeys[1], (NV,), jnp.float32, math.log(0.3), math.log(3.0)))
    return values * rising[:, None, None] * field_scale[None, :, None]


def block_scale(stream_key, shape, pieces, least, top_value):
    gain, own = 1.0, jax.random.fold_in(stream_key, 6)
    for axis_at, shards_of in pieces:
        heights = jnp.exp(jax.random.uniform(jax.random.fold_in(own, axis_at), (shards_of,), jnp.float32, least / len(pieces), top_value / len(pieces)))
        gain = gain * jnp.repeat(heights, shape[axis_at] // shards_of).reshape([-1 if axis == axis_at else 1 for axis in range(len(shape))])
    return gain


def setup_inputs(seed: int = 0) -> dict:
    key_of = jax.random.split(jax.random.key(seed), 5)
    locations = jnp.clip(1.0 * jax.random.uniform(key_of[0], (NBLK, 3, BS), jnp.float32) ** block_scale(key_of[0], (NBLK, 3, BS), ((0, 128),), -0.2, 0.2), 0.0, 1.0)
    neighbours = draw_neighbours(jax.random.fold_in(key_of[4], 71), 0)
    observations = draw_observations(jax.random.fold_in(key_of[4], 71), 0)
    noise_prec = jnp.clip(jnp.exp(math.log(4.0) - 2.0794415 * jax.random.uniform(key_of[3], (NBLK, NV, BS), jnp.float32) ** block_scale(key_of[3], (NBLK, NV, BS), ((0, 128),), -0.2, 0.2)), 0.5, 4.0)
    return dict(locations=locations, neighbours=neighbours, observations=observations, noise_prec=noise_prec)


SCALE_LENGTH = 0.5
NUGGET = 0.5
SQRT_THREE = math.sqrt(3.0)
HIGHEST = lax.Precision.HIGHEST

def kernel_factor(point_set, point_mask, own_size):
    offsets = point_set[:, :, None] - point_set[:, None, :]
    distance = jnp.sqrt(lax.optimization_barrier(jnp.sum(offsets * offsets, axis=0)))
    scaled = SQRT_THREE / SCALE_LENGTH * distance
    covariance = (1.0 + scaled) * jnp.exp(-scaled)
    order_size = point_set.shape[1]
    identity = jnp.eye(order_size, dtype=point_set.dtype)
    diagonal_term = NUGGET * point_mask + (1.0 - point_mask)
    covariance = covariance * (point_mask[:, None] * point_mask[None, :]) + identity * diagonal_term[:, None]
    factor_lower = jnp.linalg.cholesky(covariance)
    unit_tail = identity[:, order_size - own_size:]
    return lax.linalg.triangular_solve(factor_lower, unit_tail, left_side=True, lower=True, transpose_a=True)

def reference(locations, neighbours, observations, noise_prec):
    block_ids = neighbours.astype(jnp.int32)
    slot_live = (block_ids >= 0).astype(locations.dtype)
    safe_ids = jnp.maximum(block_ids, 0).astype(jnp.int32)

    def gather_slots(field):
        picked = field[safe_ids] * slot_live[:, :, None, None]
        picked = jnp.transpose(picked, (0, 2, 1, 3)).reshape(NBLK, field.shape[1], NEIGH * BS)
        return jnp.concatenate([picked, field], axis=2)
    point_sets = gather_slots(locations)
    point_mask = jnp.concatenate([jnp.repeat(slot_live, BS, axis=1), jnp.ones((NBLK, BS), locations.dtype)], axis=1)
    factors = lax.map(lambda pair: kernel_factor(pair[0], pair[1], BS), (point_sets, point_mask))

    def apply_transpose(field):
        return jnp.einsum('bvk,bkp->bvp', gather_slots(field), factors, precision=HIGHEST)

    def apply_factor(field):
        spread = jnp.einsum('bvp,bkp->bvk', field, factors, precision=HIGHEST)
        own_part = spread[:, :, NEIGH * BS:]
        slot_parts = spread[:, :, :NEIGH * BS].reshape(NBLK, NV, NEIGH, BS) * slot_live[:, None, :, None]
        slot_parts = jnp.transpose(slot_parts, (0, 2, 1, 3)).reshape(NBLK * NEIGH, NV, BS)
        return own_part + jnp.zeros_like(own_part).at[safe_ids.reshape(-1)].add(slot_parts)

    def operator(field):
        return apply_factor(apply_transpose(field)) + noise_prec * field
    solution = jnp.zeros_like(observations)
    residual = observations
    direction = observations
    norm_now = lax.optimization_barrier(jnp.sum(residual * residual, axis=(0, 2)))
    for iteration in range(ITERS):
        image = operator(direction)
        alpha = norm_now / lax.optimization_barrier(jnp.sum(direction * image, axis=(0, 2)))
        solution = solution + alpha[None, :, None] * direction
        residual = residual - alpha[None, :, None] * image
        if iteration + 1 < ITERS:
            norm_next = lax.optimization_barrier(jnp.sum(residual * residual, axis=(0, 2)))
            direction = residual + (norm_next / norm_now)[None, :, None] * direction
            norm_now = norm_next
    return (solution, residual)
```

```python
import math

import jax
import jax.numpy as jnp
import numpy as np
from jax import lax
from jax.experimental import pallas as pl
from jax.experimental.pallas import tpu as pltpu
from jax.sharding import PartitionSpec as P

SCALE_LENGTH = 0.5
NUGGET = 0.5
SQRT_THREE = math.sqrt(3.0)
F32 = jnp.float32
BF16 = jnp.bfloat16
NN = (((1,), (0,)), ((), ()))
NT = (((1,), (1,)), ((), ()))
DOUBLINGS = 7
GRP, DEV = 4, 32


def coefficients(size):
    low, high = NUGGET, size + NUGGET
    tau = (high + low) / (high - low)
    rows = []
    for _ in range(DOUBLINGS):
        twice = 2.0 * tau * tau - 1.0
        rows.append((2.0 * tau * tau / twice, 1.0 / twice))
        tau = twice
    return np.array(rows, np.float32), 2.0 / (high + low)


def split(x):
    high = x.astype(BF16)
    return high, (x - high.astype(F32)).astype(BF16)


def dot(a, b, dims=NN):
    return lax.dot_general(a, b, dims, preferred_element_type=F32)


def dot3(a, b, dims=NN):
    return dot(a[0], b[0], dims) + (dot(a[0], b[1], dims) + dot(a[1], b[0], dims))


def dot6(a, b, dims=NN):
    return lax.dot_general(
        a, b, dims, preferred_element_type=F32, precision=lax.Precision.HIGHEST
    )


def neighbourhood():
    g, d = lax.axis_index("grp"), lax.axis_index("dev")
    flat = g * DEV + d
    after, before = lax.rem(flat + 1, GRP * DEV), lax.rem(flat + GRP * DEV - 1, GRP * DEV)
    return g, d, place(after), place(before)


def place(flat):
    return {"grp": flat // DEV, "dev": lax.rem(flat, DEV)}


def greet(g, d, after, before):
    barrier = pltpu.get_barrier_semaphore()

    def one(k, carry):
        pl.semaphore_signal(
            barrier, 1, device_id={"grp": g, "dev": lax.rem(d + k, DEV)}
        )
        return carry

    lax.fori_loop(1, DEV, one, 0)
    for k in range(1, GRP):
        pl.semaphore_signal(barrier, 1, device_id={"grp": lax.rem(g + k, GRP), "dev": d})
    pl.semaphore_signal(barrier, 1, device_id=after)
    pl.semaphore_signal(barrier, 1, device_id=before)
    return barrier


def remote(src, dst, send, recv, device):
    return pltpu.make_async_remote_copy(
        src_ref=src, dst_ref=dst, send_sem=send, recv_sem=recv, device_id=device
    )


def gather_kernel(
    loc, obs, prev_loc, prev_obs, col_obs, all_loc, all_obs, col_loc, sems_s, sems_r, sem_l
):
    g, d, after, before = neighbourhood()
    barrier = greet(g, d, after, before)
    pl.semaphore_wait(barrier, DEV - 1 + GRP - 1 + 2)
    ahead = [
        remote(loc.at[0], prev_loc, sems_s.at[0], sems_r.at[0], after),
        remote(obs.at[0], prev_obs, sems_s.at[1], sems_r.at[1], after),
    ]
    column = []
    for k in range(1, GRP):
        mate = {"grp": k, "dev": d}
        column.append(remote(loc.at[0], col_loc, sems_s.at[2 * k], sems_r.at[2], mate))
        column.append(remote(obs.at[0], col_obs, sems_s.at[2 * k + 1], sems_r.at[3], mate))
    own = [
        pltpu.make_async_copy(loc.at[0], col_loc, sem_l.at[0]),
        pltpu.make_async_copy(obs.at[0], col_obs, sem_l.at[1]),
    ]

    @pl.when(g == 0)
    def _():
        for c in column + own:
            c.start()

    for c in ahead:
        c.start()

    @pl.when(g == 0)
    def _():
        for c in own:
            c.wait()

    @pl.when(g != 0)
    def _():
        column[0].wait_recv()
        column[1].wait_recv()

    mine = [
        pltpu.make_async_copy(col_loc, all_loc.at[d], sem_l.at[0]),
        pltpu.make_async_copy(col_obs, all_obs.at[d], sem_l.at[1]),
    ]
    for c in mine:
        c.start()

    def spread(k, carry):
        peer = {"grp": g, "dev": lax.rem(d + k, DEV)}
        remote(col_loc, all_loc.at[d], sems_s.at[8], sems_r.at[4], peer).start()
        remote(col_obs, all_obs.at[d], sems_s.at[9], sems_r.at[5], peer).start()
        return carry

    lax.fori_loop(1, DEV, spread, 0)
    others = pl.ds(0, DEV - 1)
    for whole, s, r in ((all_loc, 8, 4), (all_obs, 9, 5)):
        piece = whole.at[others]
        c = remote(piece, piece, sems_s.at[s], sems_r.at[r], after)
        c.wait_send()
        c.wait_recv()
    for c in mine + ahead:
        c.wait()

    @pl.when(g == 0)
    def _():
        for c in column:
            c.wait_send()


def factor_kernel(near, coef, prev_loc, all_loc, loc, g_out, p_out, tiles, low, r_ref, x_ref):
    size = loc.shape[2]
    first = coefficients(size)[1]
    live = [jnp.where(near[0, s] >= 0, 1.0, 0.0).astype(F32) for s in (0, 2, 3)] + [1.0]
    points = [
        prev_loc[...],
        all_loc[jnp.maximum(near[0, 2], 0)],
        all_loc[jnp.maximum(near[0, 3], 0)],
        loc[0],
    ]
    rows = lax.broadcasted_iota(jnp.int32, (size, size), 0)
    columns = lax.broadcasted_iota(jnp.int32, (size, size), 1)
    eye = (rows == columns).astype(F32)
    for i in range(4):
        padded = jnp.concatenate([points[i], jnp.zeros((5, size), F32)], axis=0)
        upright = padded.T
        for j in range(i + 1):
            total = None
            for c in range(3):
                offset = upright[:, c : c + 1] - points[j][c : c + 1, :]
                total = offset * offset if total is None else total + offset * offset
            scaled = (SQRT_THREE / SCALE_LENGTH) * jnp.sqrt(total)
            value = (1.0 + scaled) * jnp.exp(-scaled) * (live[i] * live[j])
            if i == j:
                value = value + eye * (NUGGET * live[i] + (1.0 - live[i]))
            tiles[i, j] = value

    def inverse(k):
        matrix = tiles[k, k]
        r = eye - first * matrix
        x_ref[...] = (first * coef[0, 0]) * (eye + r)
        pair = split(r)
        r_ref[...] = coef[0, 0] * dot3(pair, pair) - coef[0, 1] * eye

        def body(n, carry):
            pair = split(r_ref[...])
            x = x_ref[...]
            a, c = coef[n, 0], coef[n, 1]
            moved = dot3(split(x), pair)
            square = dot3(pair, pair)
            x_ref[...] = a * (x + moved)
            r_ref[...] = a * square - c * eye
            return carry

        lax.fori_loop(1, DOUBLINGS, body, 0)
        x = x_ref[...]
        left = eye - dot6(tiles[k, k], x)
        return x + dot3(split(x), split(left))

    for k in range(3):
        inv = inverse(k)
        for i in range(k + 1, 4):
            low[i, k] = dot6(tiles[i, k], inv)
        for j in range(k + 1, 4):
            for i in range(j, 4):
                tiles[i, j] = tiles[i, j] - dot6(low[i, k], tiles[j, k], NT)
    inv = inverse(3)
    p_out[0], p_out[1] = split(inv)
    g2 = -low[3, 2]
    g1 = -(low[3, 1] + dot6(g2, low[2, 1]))
    g0 = -(low[3, 0] + dot6(g1, low[1, 0]) + dot6(g2, low[2, 0]))
    for k, value in enumerate((g0, g1, g2)):
        high, rest = split(value)
        g_out[0, :, k * size : (k + 1) * size] = high
        g_out[1, :, k * size : (k + 1) * size] = rest


def lane_group(shape):
    return lax.broadcasted_iota(jnp.int32, shape, 1) // 32


def pack(parts):
    out = None
    for k, part in enumerate(parts):
        half = part[:, :128] + part[:, 128:] if part.shape[1] == 256 else part
        if half is not part:
            half = half + pltpu.roll(half, 64, 1)
            half = half + pltpu.roll(half, 32, 1)
        group = lane_group(half.shape)
        out = half if out is None else jnp.where(group == k, half, out)
    return out


def unpack(packed, k):
    return jnp.sum(
        jnp.where(lane_group(packed.shape) == k, packed, 0.0), axis=1, keepdims=True
    )


def solve_kernel(
    near, obs, noise, g_mat, p_mat, prev_obs, col_obs, all_obs,
    sol_out, res_out,
    msg, rs1, rs2, x1, x2, back1, back2, hop, ag, rcol, prev1, stage, sems_s, sems_r,
):
    size = obs.shape[2]
    g, d, after, before = neighbourhood()
    barrier = greet(g, d, after, before)
    first_group = jnp.where(g == 0, 1.0, 0.0).astype(F32)
    wi, wj = near[0, 2], near[0, 3]
    b = obs[0]
    prec = noise[0]
    others = pl.ds(0, DEV - 1)

    def dot_small(rows, mat, dims):
        high, rest = split(rows)
        return dot(high, mat[0], dims) + (dot(high, mat[1], dims) + dot(rest, mat[0], dims))

    def apply(own, before_rows, table):
        slots = jnp.concatenate(
            [before_rows, table[jnp.maximum(wi, 0)], table[jnp.maximum(wj, 0)]], axis=1
        )
        v = own + dot_small(slots, g_mat, NT)
        w = dot_small(v, p_mat, NN)
        return v, w, dot_small(w, g_mat, NN)

    def scatter(u, packed, recv, back, k):
        hop[k] = u[:, :size]
        ui, uj = u[:, size : 2 * size], u[:, 2 * size :]

        def fill(m, carry):
            fi = jnp.where(wi == m, 1.0, 0.0).astype(F32)
            fj = jnp.where(wj == m, 1.0, 0.0).astype(F32)
            msg[k, m, :, :size] = fi * ui + fj * uj
            msg[k, m, :, size:] = packed
            return carry

        lax.fori_loop(0, DEV, fill, 0)
        if k == 0:
            pl.semaphore_wait(barrier, DEV - 1 + GRP - 1 + 2)
        returned = remote(hop.at[k], back, sems_s.at[0], sems_r.at[k], before)
        returned.start()
        mine = pltpu.make_async_copy(msg.at[k, d], recv.at[d], sems_s.at[1])
        mine.start()

        def spread(n, carry):
            m = lax.rem(d + n, DEV)
            remote(
                msg.at[k, m], recv.at[d], sems_s.at[2], sems_r.at[2 + k], {"grp": g, "dev": m}
            ).start()
            return carry

        lax.fori_loop(1, DEV, spread, 0)
        piece = recv.at[others]
        every = remote(piece, piece, sems_s.at[2], sems_r.at[2 + k], after)
        every.wait_recv()
        mine.wait()
        returned.wait()
        total = recv[0]
        for n in range(1, DEV):
            total = total + recv[n]
        every.wait_send()
        return total, back[...]

    def across(value, recv, k):
        recv[g] = value
        stage[k] = value
        src = stage.at[k]
        copies = [
            remote(
                src, recv.at[g], sems_s.at[2 + n + 3 * k], sems_r.at[3 + n + 3 * k],
                {"grp": lax.rem(g + n, GRP), "dev": d},
            )
            for n in range(1, GRP)
        ]
        for c in copies:
            c.start()

        for c in copies:
            c.wait()
        return (recv[0] + recv[1]) + (recv[2] + recv[3])

    v0, w0, u0 = apply(b, prev_obs[...], all_obs)
    kept = prec * b
    packed = pack([b * b, v0 * w0 + kept * b])
    total, returned = scatter(u0, packed, rs1, back1, 0)
    own = w0 + kept + returned
    total = jnp.concatenate([total[:, :size] + first_group * own, total[:, size:]], axis=1)
    total = across(total, x1, 0)
    column = total[:, :size]
    rr0, p0 = unpack(total[:, size:], 0), unpack(total[:, size:], 1)
    alpha0 = rr0 / p0
    image0 = jnp.where(g == 0, column, own)
    r1 = b - alpha0 * image0
    rcol[0] = r1
    rcol[1] = col_obs[...] - alpha0 * column
    ahead = remote(rcol.at[0], prev1, sems_s.at[0], sems_r.at[10], after)
    ahead.start()
    mine = pltpu.make_async_copy(rcol.at[1], ag.at[d], sems_s.at[1])
    mine.start()

    def spread(n, carry):
        peer = {"grp": g, "dev": lax.rem(d + n, DEV)}
        remote(rcol.at[1], ag.at[d], sems_s.at[2], sems_r.at[11], peer).start()
        return carry

    lax.fori_loop(1, DEV, spread, 0)
    piece = ag.at[others]
    every = remote(piece, piece, sems_s.at[2], sems_r.at[11], after)
    ahead.wait()
    mine.wait()
    every.wait()
    v1, w1, u1 = apply(r1, prev1[...], ag)
    kept = prec * r1
    packed = pack([v1 * w1 + kept * r1, v1 * w0 + kept * b, r1 * r1])
    total, returned = scatter(u1, packed, rs2, back2, 1)
    own = w1 + kept + returned
    total = jnp.concatenate([total[:, :size] + first_group * own, total[:, size:]], axis=1)
    total = across(total, x2, 1)
    s1, s2, rr1 = (unpack(total[:, size:], k) for k in range(3))
    beta = rr1 / rr0
    alpha1 = rr1 / (s1 + 2.0 * beta * s2 + beta * beta * p0)
    image1 = jnp.where(g == 0, total[:, :size], own) + beta * image0
    sol_out[0] = alpha0 * b + alpha1 * (r1 + beta * b)
    res_out[0] = r1 - alpha1 * image1


def local(locations, neighbours, observations, noise_prec):
    points, fields = locations.shape[2], observations.shape[1]
    vmem = pl.BlockSpec(memory_space=pltpu.VMEM)
    smem = pl.BlockSpec(memory_space=pltpu.SMEM)
    shape = jax.ShapeDtypeStruct
    prev_loc, prev_obs, col_obs, all_loc, all_obs = pl.pallas_call(
        gather_kernel,
        out_shape=(
            shape((3, points), F32),
            shape((fields, points), F32),
            shape((fields, points), F32),
            shape((DEV, 3, points), F32),
            shape((DEV, fields, points), F32),
        ),
        in_specs=[vmem] * 2,
        out_specs=(vmem,) * 5,
        scratch_shapes=[
            pltpu.VMEM((3, points), F32),
            pltpu.SemaphoreType.DMA((10,)),
            pltpu.SemaphoreType.DMA((6,)),
            pltpu.SemaphoreType.DMA((2,)),
        ],
        compiler_params=pltpu.CompilerParams(collective_id=0, has_side_effects=True),
    )(locations, observations)
    g_mat, p_mat = pl.pallas_call(
        factor_kernel,
        out_shape=(shape((2, points, 3 * points), BF16), shape((2, points, points), BF16)),
        in_specs=[smem, smem, vmem, vmem, vmem],
        out_specs=(vmem,) * 2,
        scratch_shapes=[
            pltpu.VMEM((4, 4, points, points), F32),
            pltpu.VMEM((4, 3, points, points), F32),
            pltpu.VMEM((points, points), F32),
            pltpu.VMEM((points, points), F32),
        ],
        compiler_params=pltpu.CompilerParams(vmem_limit_bytes=40 << 20),
    )(neighbours, jnp.asarray(coefficients(points)[0]), prev_loc, all_loc, locations)
    wide = points + 128
    return pl.pallas_call(
        solve_kernel,
        out_shape=(shape((1, fields, points), F32),) * 2,
        in_specs=[smem] + [vmem] * 7,
        out_specs=(vmem,) * 2,
        scratch_shapes=[
            pltpu.VMEM((2, DEV, fields, wide), F32),
            pltpu.VMEM((DEV, fields, wide), F32),
            pltpu.VMEM((DEV, fields, wide), F32),
            pltpu.VMEM((GRP, fields, wide), F32),
            pltpu.VMEM((GRP, fields, wide), F32),
            pltpu.VMEM((fields, points), F32),
            pltpu.VMEM((fields, points), F32),
            pltpu.VMEM((2, fields, points), F32),
            pltpu.VMEM((DEV, fields, points), F32),
            pltpu.VMEM((2, fields, points), F32),
            pltpu.VMEM((fields, points), F32),
            pltpu.VMEM((2, fields, wide), F32),
            pltpu.SemaphoreType.DMA((9,)),
            pltpu.SemaphoreType.DMA((12,)),
        ],
        compiler_params=pltpu.CompilerParams(
            collective_id=1, has_side_effects=True, vmem_limit_bytes=40 << 20
        ),
    )(neighbours, observations, noise_prec, g_mat, p_mat, prev_obs, col_obs, all_obs)


def solution(mesh):
    placed = (
        P(("grp", "dev"), None, None),
        P(("grp", "dev"), None),
        P(("grp", "dev"), None, None),
        P(("grp", "dev"), None, None),
    )
    return jax.shard_map(
        local,
        mesh=mesh,
        in_specs=placed,
        out_specs=(P(("grp", "dev"), None, None), P(("grp", "dev"), None, None)),
        check_vma=False,
    )
```

```python
import math

import jax
import jax.numpy as jnp
from jax import lax
from jax.experimental import pallas as pl
from jax.experimental.pallas import tpu as pltpu
from jax.sharding import PartitionSpec as P

SCALE_LENGTH = 0.5
NUGGET = 0.5
SQRT_THREE = math.sqrt(3.0)
F32 = jnp.float32
BF16 = jnp.bfloat16
NN = (((1,), (0,)), ((), ()))
NT = (((1,), (1,)), ((), ()))
DOUBLINGS = 7
GRP, DEV = 4, 32


def coefficients(size):
    low, high = NUGGET, size + NUGGET
    tau = (high + low) / (high - low)
    rows = []
    for _ in range(DOUBLINGS):
        twice = 2.0 * tau * tau - 1.0
        rows.append((2.0 * tau * tau / twice, 1.0 / twice))
        tau = twice
    return rows, 2.0 / (high + low)


def pick(values, n):
    out = jnp.float32(values[-1])
    for k in range(len(values) - 2, -1, -1):
        out = jnp.where(n == k, jnp.float32(values[k]), out)
    return out


def split(x):
    high = x.astype(BF16)
    return high, (x - high.astype(F32)).astype(BF16)


def dot(a, b, dims=NN):
    return lax.dot_general(a, b, dims, preferred_element_type=F32)


def dot3(a, b, dims=NN):
    return dot(a[0], b[0], dims) + (dot(a[0], b[1], dims) + dot(a[1], b[0], dims))


def dot6(a, b, dims=NN):
    return lax.dot_general(
        a, b, dims, preferred_element_type=F32, precision=lax.Precision.HIGHEST
    )


def neighbourhood():
    g, d = lax.axis_index("grp"), lax.axis_index("dev")
    flat = g * DEV + d
    after, before = lax.rem(flat + 1, GRP * DEV), lax.rem(flat + GRP * DEV - 1, GRP * DEV)
    return g, d, place(after), place(before)


def place(flat):
    return {"grp": flat // DEV, "dev": lax.rem(flat, DEV)}


def greet(g, d, after, before):
    barrier = pltpu.get_barrier_semaphore()

    def one(k, carry):
        pl.semaphore_signal(
            barrier, 1, device_id={"grp": g, "dev": lax.rem(d + k, DEV)}
        )
        return carry

    lax.fori_loop(1, DEV, one, 0)
    for k in range(1, GRP):
        pl.semaphore_signal(barrier, 1, device_id={"grp": lax.rem(g + k, GRP), "dev": d})
    pl.semaphore_signal(barrier, 1, device_id=after)
    pl.semaphore_signal(barrier, 1, device_id=before)
    return barrier


def remote(src, dst, send, recv, device):
    return pltpu.make_async_remote_copy(
        src_ref=src, dst_ref=dst, send_sem=send, recv_sem=recv, device_id=device
    )


def lane(shape):
    return lax.broadcasted_iota(jnp.int32, shape, 1)


def sublane(shape):
    return lax.broadcasted_iota(jnp.int32, shape, 0)


def to_row(parts):
    fields = parts[0].shape[0]
    spread = jnp.zeros((fields, 128), F32)
    slot = lane(spread.shape) - sublane(spread.shape)
    for k, part in enumerate(parts):
        spread = jnp.where(slot == k * fields, jnp.sum(part, axis=1, keepdims=True), spread)
    return jnp.sum(spread, axis=0, keepdims=True)


def from_row(row, k, fields):
    spread = jnp.broadcast_to(row, (fields, 128))
    slot = lane(spread.shape) - sublane(spread.shape)
    return jnp.sum(jnp.where(slot == k * fields, spread, 0.0), axis=1, keepdims=True)


def kernel(
    near, loc, obs, noise,
    sol_out, res_out,
    loc_v, obs_v, noise_v, prev_loc, prev_obs, col_loc, col_obs, all_loc, all_obs,
    tiles, low, r_ref, x_ref, g_mat, p_mat,
    msg, rs, xs, stage, hop, back, rcol, prev1, ag,
    sem_in, sem_mine, sem_s, sem_r,
):
    fields, size = obs_v.shape
    g, d, after, before = neighbourhood()
    barrier = greet(g, d, after, before)
    incoming = [
        pltpu.make_async_copy(src, dst, sem_in.at[k])
        for k, (src, dst) in enumerate(((loc, loc_v), (obs.at[0], obs_v), (noise.at[0], noise_v)))
    ]
    for c in incoming:
        c.start()
    others = pl.ds(0, DEV - 1)
    eye = (sublane((size, size)) == lane((size, size))).astype(F32)
    rows, first = coefficients(size)
    first_group = jnp.where(g == 0, 1.0, 0.0).astype(F32)
    wi, wj = near[0, 2], near[0, 3]
    live = [jnp.where(near[0, s] >= 0, 1.0, 0.0).astype(F32) for s in (0, 2, 3)] + [1.0]

    def points(value):
        flat = [value[c] for c in range(3)]
        upright = jnp.concatenate(flat + [jnp.zeros((5, size), F32)], axis=0).T
        return flat, upright

    def covariance(i, j):
        total = None
        for c in range(3):
            offset = pts[i][1][:, c : c + 1] - pts[j][0][c]
            total = offset * offset if total is None else total + offset * offset
        scaled = (SQRT_THREE / SCALE_LENGTH) * jnp.sqrt(total)
        value = (1.0 + scaled) * jnp.exp(-scaled) * (live[i] * live[j])
        if i == j:
            value = value + eye * (NUGGET * live[i] + (1.0 - live[i]))
        tiles[i, j] = value

    def spread(src, dst, s, r):
        def one(n, carry):
            peer = {"grp": g, "dev": lax.rem(d + n, DEV)}
            remote(src, dst.at[d], sem_s.at[s], sem_r.at[r], peer).start()
            return carry

        lax.fori_loop(1, DEV, one, 0)
        piece = dst.at[others]
        return remote(piece, piece, sem_s.at[s], sem_r.at[r], after)

    def local_copy(src, dst, k):
        c = pltpu.make_async_copy(src, dst, sem_mine.at[k])
        c.start()
        return c

    incoming[0].wait()
    pts = [None, None, None, points(loc_v)]
    covariance(3, 3)
    pl.semaphore_wait(barrier, DEV - 1 + GRP - 1 + 2)
    ahead_loc = remote(loc_v, prev_loc, sem_s.at[0], sem_r.at[0], after)
    column_loc = [
        remote(loc_v, col_loc, sem_s.at[1 + k], sem_r.at[1], {"grp": k, "dev": d})
        for k in range(1, GRP)
    ]
    own_loc = pltpu.make_async_copy(loc_v, col_loc, sem_mine.at[0])

    @pl.when(g == 0)
    def _():
        for c in column_loc:
            c.start()
        own_loc.start()

    ahead_loc.start()
    incoming[1].wait()
    incoming[2].wait()
    ahead_obs = remote(obs_v, prev_obs, sem_s.at[5], sem_r.at[2], after)
    column_obs = [
        remote(obs_v, col_obs, sem_s.at[5 + k], sem_r.at[3], {"grp": k, "dev": d})
        for k in range(1, GRP)
    ]
    own_obs = pltpu.make_async_copy(obs_v, col_obs, sem_mine.at[1])
    ahead_obs.start()

    @pl.when(g == 0)
    def _():
        for c in column_obs:
            c.start()
        own_obs.start()

    ahead_loc.wait()
    pts[0] = points(prev_loc)
    covariance(0, 0)

    @pl.when(g == 0)
    def _():
        own_loc.wait()

    @pl.when(g != 0)
    def _():
        column_loc[0].wait_recv()

    mine_loc = local_copy(col_loc, all_loc.at[d], 2)
    every_loc = spread(col_loc, all_loc, 9, 4)

    def inverse(k):
        r = eye - first * tiles[k, k]
        x_ref[...] = (first * rows[0][0]) * (eye + r)
        pair = split(r)
        r_ref[...] = rows[0][0] * dot3(pair, pair) - rows[0][1] * eye

        def body(n, carry):
            pair = split(r_ref[...])
            x = x_ref[...]
            a, c = pick([row[0] for row in rows], n), pick([row[1] for row in rows], n)
            moved = dot3(split(x), pair)
            square = dot3(pair, pair)
            x_ref[...] = a * (x + moved)
            r_ref[...] = a * square - c * eye
            return carry

        lax.fori_loop(1, DOUBLINGS, body, 0)
        x = x_ref[...]
        left = eye - dot6(tiles[k, k], x)
        return x + dot3(split(x), split(left))

    inv = inverse(0)
    covariance(3, 0)
    low[3, 0] = dot6(tiles[3, 0], inv)
    tiles[3, 3] = tiles[3, 3] - dot6(low[3, 0], tiles[3, 0], NT)

    @pl.when(g == 0)
    def _():
        own_obs.wait()

    @pl.when(g != 0)
    def _():
        column_obs[0].wait_recv()

    mine_loc.wait()
    every_loc.wait_recv()
    mine_obs = local_copy(col_obs, all_obs.at[d], 3)
    every_obs = spread(col_obs, all_obs, 10, 5)
    pts[1] = points(all_loc[jnp.maximum(wi, 0)])
    pts[2] = points(all_loc[jnp.maximum(wj, 0)])
    for i, j in ((1, 0), (1, 1), (2, 0), (2, 1), (2, 2), (3, 1), (3, 2)):
        covariance(i, j)
    for k in range(3):
        if k:
            inv = inverse(k)
        for i in range(k + 1, 4):
            if (i, k) != (3, 0):
                low[i, k] = dot6(tiles[i, k], inv)
        for j in range(k + 1, 4):
            for i in range(j, 4):
                if (i, j, k) != (3, 3, 0):
                    tiles[i, j] = tiles[i, j] - dot6(low[i, k], tiles[j, k], NT)
    inv = inverse(3)
    p_mat[0], p_mat[1] = split(inv)
    g2 = -low[3, 2]
    g1 = -(low[3, 1] + dot6(g2, low[2, 1]))
    g0 = -(low[3, 0] + dot6(g1, low[1, 0]) + dot6(g2, low[2, 0]))
    for k, value in enumerate((g0, g1, g2)):
        high, rest = split(value)
        g_mat[0, :, k * size : (k + 1) * size] = high
        g_mat[1, :, k * size : (k + 1) * size] = rest

    def dot_small(rows, mat, dims):
        high, rest = split(rows)
        return dot(high, mat[0], dims) + (dot(high, mat[1], dims) + dot(rest, mat[0], dims))

    def apply(own, before_rows, table):
        slots = jnp.concatenate(
            [before_rows, table[jnp.maximum(wi, 0)], table[jnp.maximum(wj, 0)]], axis=1
        )
        v = own + dot_small(slots, g_mat, NT)
        w = dot_small(v, p_mat, NN)
        return v, w, dot_small(w, g_mat, NN)

    def reduce(u, own, row, k):
        hop[k] = u[:, :size]
        half = size // 2
        ui, uj = u[:, size : 2 * size], u[:, 2 * size :]

        def fill(m, carry):
            fi = jnp.where(wi == m, 1.0, 0.0).astype(F32)
            fj = jnp.where(wj == m, 1.0, 0.0).astype(F32)
            block = fi * ui + fj * uj
            msg[k, m, :fields] = block[:, :half]
            msg[k, m, fields : 2 * fields] = block[:, half:]
            msg[k, m, 2 * fields :] = row
            return carry

        lax.fori_loop(0, DEV, fill, 0)
        returned = remote(hop.at[k], back.at[k], sem_s.at[11], sem_r.at[6 + k], before)
        returned.start()
        mine = local_copy(msg.at[k, d], rs.at[k, d], 0)

        def one(n, carry):
            m = lax.rem(d + n, DEV)
            remote(
                msg.at[k, m], rs.at[k, d], sem_s.at[12], sem_r.at[8 + k], {"grp": g, "dev": m}
            ).start()
            return carry

        lax.fori_loop(1, DEV, one, 0)
        piece = rs.at[k, others]
        every = remote(piece, piece, sem_s.at[12], sem_r.at[8 + k], after)
        returned.wait()
        own = own + back[k]
        every.wait_recv()
        mine.wait()
        total = rs[k, 0]
        for n in range(1, DEV):
            total = total + rs[k, n]
        held = first_group * jnp.concatenate(
            [own[:, :half], own[:, half:], jnp.zeros((1, half), F32)], axis=0
        )
        total = total + held
        xs[k, g] = total
        stage[k] = total
        copies = [
            remote(
                stage.at[k], xs.at[k, g], sem_s.at[12 + n], sem_r.at[9 + n + 3 * k],
                {"grp": lax.rem(g + n, GRP), "dev": d},
            )
            for n in range(1, GRP)
        ]
        for c in copies:
            c.start()
        every.wait_send()
        for c in copies:
            c.wait()
        total = (xs[k, 0] + xs[k, 1]) + (xs[k, 2] + xs[k, 3])
        column = jnp.concatenate([total[:fields], total[fields : 2 * fields]], axis=1)
        image = jnp.where(g == 0, column, own)
        return image, column, total[2 * fields :]

    ahead_obs.wait()
    mine_obs.wait()
    every_obs.wait_recv()
    b, prec = obs_v[...], noise_v[...]
    v0, w0, u0 = apply(b, prev_obs[...], all_obs)
    kept = prec * b
    image0, column, row = reduce(u0, w0 + kept, to_row([b * b, v0 * w0 + kept * b]), 0)
    rr0, p0 = from_row(row, 0, fields), from_row(row, 1, fields)
    alpha0 = rr0 / p0
    r1 = b - alpha0 * image0
    rcol[0] = r1
    rcol[1] = col_obs[...] - alpha0 * column
    ahead = remote(rcol.at[0], prev1, sem_s.at[11], sem_r.at[16], after)
    ahead.start()
    mine = local_copy(rcol.at[1], ag.at[d], 0)
    every = spread(rcol.at[1], ag, 12, 17)
    ahead.wait()
    mine.wait()
    every.wait()
    v1, w1, u1 = apply(r1, prev1[...], ag)
    kept = prec * r1
    image1, column, row = reduce(
        u1, w1 + kept, to_row([v1 * w1 + kept * r1, v1 * w0 + kept * b, r1 * r1]), 1
    )
    s1, s2, rr1 = (from_row(row, k, fields) for k in range(3))
    beta = rr1 / rr0
    alpha1 = rr1 / (s1 + 2.0 * beta * s2 + beta * beta * p0)
    image1 = image1 + beta * image0
    sol_out[0] = alpha0 * b + alpha1 * (r1 + beta * b)
    res_out[0] = r1 - alpha1 * image1
    every_loc.wait_send()
    every_obs.wait_send()

    @pl.when(g == 0)
    def _():
        for c in column_loc + column_obs:
            c.wait_send()


def local(locations, neighbours, observations, noise_prec):
    points, fields = locations.shape[2], observations.shape[1]
    vmem = pl.BlockSpec(memory_space=pltpu.VMEM)
    smem = pl.BlockSpec(memory_space=pltpu.SMEM)
    hbm = pl.BlockSpec(memory_space=pltpu.HBM)

    def f32(*shape):
        return pltpu.VMEM(shape, F32)

    tall = 2 * fields + 1
    return pl.pallas_call(
        kernel,
        out_shape=(jax.ShapeDtypeStruct((1, fields, points), F32),) * 2,
        in_specs=[smem, hbm, hbm, hbm],
        out_specs=(vmem,) * 2,
        scratch_shapes=[
            f32(3, 1, points), f32(fields, points), f32(fields, points),
            f32(3, 1, points), f32(fields, points),
            f32(3, 1, points), f32(fields, points),
            f32(DEV, 3, 1, points), f32(DEV, fields, points),
            f32(4, 4, points, points), f32(4, 3, points, points),
            f32(points, points), f32(points, points),
            pltpu.VMEM((2, points, 3 * points), BF16), pltpu.VMEM((2, points, points), BF16),
            f32(2, DEV, tall, points // 2), f32(2, DEV, tall, points // 2),
            f32(2, GRP, tall, points // 2), f32(2, tall, points // 2),
            f32(2, fields, points), f32(2, fields, points),
            f32(2, fields, points), f32(fields, points), f32(DEV, fields, points),
            pltpu.SemaphoreType.DMA((3,)),
            pltpu.SemaphoreType.DMA((4,)),
            pltpu.SemaphoreType.DMA((16,)),
            pltpu.SemaphoreType.DMA((18,)),
        ],
        compiler_params=pltpu.CompilerParams(
            collective_id=0, has_side_effects=True, vmem_limit_bytes=48 << 20
        ),
    )(neighbours, jnp.transpose(locations, (1, 0, 2)), observations, noise_prec)


def solution(mesh):
    placed = (
        P(("grp", "dev"), None, None),
        P(("grp", "dev"), None),
        P(("grp", "dev"), None, None),
        P(("grp", "dev"), None, None),
    )
    return jax.shard_map(
        local,
        mesh=mesh,
        in_specs=placed,
        out_specs=(P(("grp", "dev"), None, None), P(("grp", "dev"), None, None)),
        check_vma=False,
    )
```

```python
import math

import jax
import jax.numpy as jnp
from jax import lax
from jax.experimental import pallas as pl
from jax.experimental.pallas import tpu as pltpu
from jax.sharding import PartitionSpec as P

SCALE_LENGTH = 0.5
NUGGET = 0.5
SQRT_THREE = math.sqrt(3.0)
F32 = jnp.float32
BF16 = jnp.bfloat16
NN = (((1,), (0,)), ((), ()))
NT = (((1,), (1,)), ((), ()))
DOUBLINGS = 7
GRP, DEV = 4, 32


def coefficients(size):
    low, high = NUGGET, size + NUGGET
    tau = (high + low) / (high - low)
    rows = []
    for _ in range(DOUBLINGS):
        twice = 2.0 * tau * tau - 1.0
        rows.append((2.0 * tau * tau / twice, 1.0 / twice))
        tau = twice
    return rows, 2.0 / (high + low)


def pick(values, n):
    out = jnp.float32(values[-1])
    for k in range(len(values) - 2, -1, -1):
        out = jnp.where(n == k, jnp.float32(values[k]), out)
    return out


def split(x):
    high = x.astype(BF16)
    return high, (x - high.astype(F32)).astype(BF16)


def dot(a, b, dims=NN):
    return lax.dot_general(a, b, dims, preferred_element_type=F32)


def dot3(a, b, dims=NN):
    return dot(a[0], b[0], dims) + (dot(a[0], b[1], dims) + dot(a[1], b[0], dims))


def dot6(a, b, dims=NN):
    return lax.dot_general(
        a, b, dims, preferred_element_type=F32, precision=lax.Precision.HIGHEST
    )


def neighbourhood():
    g, d = lax.axis_index("grp"), lax.axis_index("dev")
    flat = g * DEV + d
    after, before = lax.rem(flat + 1, GRP * DEV), lax.rem(flat + GRP * DEV - 1, GRP * DEV)
    return g, d, place(after), place(before)


def mates(d):
    far = (2, 1, 3, 0)
    y, z, c = d // 8, lax.rem(d // 2, 4), lax.rem(d, 2)
    ys = {k: lax.rem(y + k, 4) * 8 for k in far}
    zs = {k: lax.rem(z + k, 4) * 2 for k in far}
    cs = {1: 1 - c, 0: c}
    return [ys[a] + (zs[b] + cs[e]) for a in far for b in far for e in (1, 0)][:-1]


def place(flat):
    return {"grp": flat // DEV, "dev": lax.rem(flat, DEV)}


def greet(g, d, after, before):
    barrier = pltpu.get_barrier_semaphore()

    def one(k, carry):
        pl.semaphore_signal(
            barrier, 1, device_id={"grp": g, "dev": lax.rem(d + k, DEV)}
        )
        return carry

    lax.fori_loop(1, DEV, one, 0)
    for k in range(1, GRP):
        pl.semaphore_signal(barrier, 1, device_id={"grp": lax.rem(g + k, GRP), "dev": d})
    pl.semaphore_signal(barrier, 1, device_id=after)
    pl.semaphore_signal(barrier, 1, device_id=before)
    return barrier


def remote(src, dst, send, recv, device):
    return pltpu.make_async_remote_copy(
        src_ref=src, dst_ref=dst, send_sem=send, recv_sem=recv, device_id=device
    )


def lane(shape):
    return lax.broadcasted_iota(jnp.int32, shape, 1)


def sublane(shape):
    return lax.broadcasted_iota(jnp.int32, shape, 0)


def to_row(parts):
    fields = parts[0].shape[0]
    spread = jnp.zeros((fields, 128), F32)
    slot = lane(spread.shape) - sublane(spread.shape)
    for k, part in enumerate(parts):
        spread = jnp.where(slot == k * fields, jnp.sum(part, axis=1, keepdims=True), spread)
    return jnp.sum(spread, axis=0, keepdims=True)


def from_row(row, k, fields):
    spread = jnp.broadcast_to(row, (fields, 128))
    slot = lane(spread.shape) - sublane(spread.shape)
    return jnp.sum(jnp.where(slot == k * fields, spread, 0.0), axis=1, keepdims=True)


def kernel(
    near_hbm, loc, obs, noise,
    out,
    near, loc_v, obs_v, noise_v, prev_loc, prev_obs, col_loc, col_obs, all_loc, all_obs,
    tiles, low, r_ref, x_ref, g_mat, p_mat,
    msg, rs, xs, stage, hop, back, rcol, prev1, ag,
    sem_in, sem_mine, sem_s, sem_r,
):
    fields, size = obs_v.shape
    g, d, after, before = neighbourhood()
    barrier = greet(g, d, after, before)
    incoming = [
        pltpu.make_async_copy(src, dst, sem_in.at[k])
        for k, (src, dst) in enumerate(
            ((loc, loc_v), (near_hbm, near), (obs.at[0], obs_v), (noise.at[0], noise_v))
        )
    ]
    for c in incoming:
        c.start()
    others = pl.ds(0, DEV - 1)
    plane = mates(d)
    eye = (sublane((size, size)) == lane((size, size))).astype(F32)
    rows, first = coefficients(size)
    first_group = jnp.where(g == 0, 1.0, 0.0).astype(F32)
    def points(value):
        flat = [value[c] for c in range(3)]
        upright = jnp.concatenate(flat + [jnp.zeros((5, size), F32)], axis=0).T
        return flat, upright

    def covariance(i, j):
        total = None
        for c in range(3):
            offset = pts[i][1][:, c : c + 1] - pts[j][0][c]
            total = offset * offset if total is None else total + offset * offset
        scaled = (SQRT_THREE / SCALE_LENGTH) * jnp.sqrt(total)
        value = (1.0 + scaled) * jnp.exp(-scaled) * (live[i] * live[j])
        if i == j:
            value = value + eye * (NUGGET * live[i] + (1.0 - live[i]))
        tiles[i, j] = value

    def spread(src, dst, s, r):
        for m in plane:
            remote(src, dst.at[d], sem_s.at[s], sem_r.at[r], {"grp": g, "dev": m}).start()
        piece = dst.at[others]
        return remote(piece, piece, sem_s.at[s], sem_r.at[r], after)

    def local_copy(src, dst, k):
        c = pltpu.make_async_copy(src, dst, sem_mine.at[k])
        c.start()
        return c

    incoming[0].wait()
    incoming[1].wait()
    wi, wj = near[0, 2], near[0, 3]
    live = [jnp.where(near[0, s] >= 0, 1.0, 0.0).astype(F32) for s in (0, 2, 3)] + [1.0]
    pts = [None, None, None, points(loc_v)]
    covariance(3, 3)
    pl.semaphore_wait(barrier, DEV - 1 + GRP - 1 + 2)
    ahead_loc = remote(loc_v, prev_loc, sem_s.at[0], sem_r.at[0], after)
    column_loc = [
        remote(loc_v, col_loc, sem_s.at[1 + k], sem_r.at[1], {"grp": k, "dev": d})
        for k in range(1, GRP)
    ]
    own_loc = pltpu.make_async_copy(loc_v, col_loc, sem_mine.at[0])

    @pl.when(g == 0)
    def _():
        for c in column_loc:
            c.start()
        own_loc.start()

    ahead_loc.start()
    incoming[2].wait()
    incoming[3].wait()
    ahead_obs = remote(obs_v, prev_obs, sem_s.at[5], sem_r.at[2], after)
    column_obs = [
        remote(obs_v, col_obs, sem_s.at[5 + k], sem_r.at[3], {"grp": k, "dev": d})
        for k in range(1, GRP)
    ]
    own_obs = pltpu.make_async_copy(obs_v, col_obs, sem_mine.at[1])
    ahead_obs.start()

    @pl.when(g == 0)
    def _():
        for c in column_obs:
            c.start()
        own_obs.start()

    ahead_loc.wait()
    pts[0] = points(prev_loc)
    covariance(0, 0)

    @pl.when(g == 0)
    def _():
        own_loc.wait()

    @pl.when(g != 0)
    def _():
        column_loc[0].wait_recv()

    mine_loc = local_copy(col_loc, all_loc.at[d], 2)
    every_loc = spread(col_loc, all_loc, 9, 4)

    def inverse(k):
        r = eye - first * tiles[k, k]
        x_ref[...] = (first * rows[0][0]) * (eye + r)
        pair = split(r)
        r_ref[...] = rows[0][0] * dot3(pair, pair) - rows[0][1] * eye

        def body(n, carry):
            pair = split(r_ref[...])
            x = x_ref[...]
            a, c = pick([row[0] for row in rows], n), pick([row[1] for row in rows], n)
            moved = dot3(split(x), pair)
            square = dot3(pair, pair)
            x_ref[...] = a * (x + moved)
            r_ref[...] = a * square - c * eye
            return carry

        lax.fori_loop(1, DOUBLINGS, body, 0)
        x = x_ref[...]
        left = eye - dot6(tiles[k, k], x)
        return x + dot3(split(x), split(left))

    inv = inverse(0)
    covariance(3, 0)
    low[3, 0] = dot6(tiles[3, 0], inv)
    tiles[3, 3] = tiles[3, 3] - dot6(low[3, 0], tiles[3, 0], NT)

    @pl.when(g == 0)
    def _():
        own_obs.wait()

    @pl.when(g != 0)
    def _():
        column_obs[0].wait_recv()

    mine_loc.wait()
    every_loc.wait_recv()
    mine_obs = local_copy(col_obs, all_obs.at[d], 3)
    every_obs = spread(col_obs, all_obs, 10, 5)
    pts[1] = points(all_loc[jnp.maximum(wi, 0)])
    pts[2] = points(all_loc[jnp.maximum(wj, 0)])
    for i, j in ((1, 0), (1, 1), (2, 0), (2, 1), (2, 2), (3, 1), (3, 2)):
        covariance(i, j)
    for k in range(3):
        if k:
            inv = inverse(k)
        for i in range(k + 1, 4):
            if (i, k) != (3, 0):
                low[i, k] = dot6(tiles[i, k], inv)
        for j in range(k + 1, 4):
            for i in range(j, 4):
                if (i, j, k) != (3, 3, 0):
                    tiles[i, j] = tiles[i, j] - dot6(low[i, k], tiles[j, k], NT)
    inv = inverse(3)
    p_mat[0], p_mat[1] = split(inv)
    g2 = -low[3, 2]
    g1 = -(low[3, 1] + dot6(g2, low[2, 1]))
    g0 = -(low[3, 0] + dot6(g1, low[1, 0]) + dot6(g2, low[2, 0]))
    for k, value in enumerate((g0, g1, g2)):
        high, rest = split(value)
        g_mat[0, :, k * size : (k + 1) * size] = high
        g_mat[1, :, k * size : (k + 1) * size] = rest

    def dot_small(rows, mat, dims):
        high, rest = split(rows)
        return dot(high, mat[0], dims) + (dot(high, mat[1], dims) + dot(rest, mat[0], dims))

    def apply(own, before_rows, table):
        slots = jnp.concatenate(
            [before_rows, table[jnp.maximum(wi, 0)], table[jnp.maximum(wj, 0)]], axis=1
        )
        v = own + dot_small(slots, g_mat, NT)
        w = dot_small(v, p_mat, NN)
        return v, w, dot_small(w, g_mat, NN)

    def reduce(u, own, row, k):
        hop[k] = u[:, :size]
        half = size // 2
        ui, uj = u[:, size : 2 * size], u[:, 2 * size :]

        def fill(m, carry):
            fi = jnp.where(wi == m, 1.0, 0.0).astype(F32)
            fj = jnp.where(wj == m, 1.0, 0.0).astype(F32)
            block = fi * ui + fj * uj
            msg[k, m, :fields] = block[:, :half]
            msg[k, m, fields : 2 * fields] = block[:, half:]
            msg[k, m, 2 * fields :] = row
            return carry

        lax.fori_loop(0, DEV, fill, 0)
        returned = remote(hop.at[k], back.at[k], sem_s.at[11], sem_r.at[6 + k], before)
        returned.start()
        mine = local_copy(msg.at[k, d], rs.at[k, d], 0)

        for m in plane:
            remote(
                msg.at[k, m], rs.at[k, d], sem_s.at[12], sem_r.at[8 + k], {"grp": g, "dev": m}
            ).start()
        piece = rs.at[k, others]
        every = remote(piece, piece, sem_s.at[12], sem_r.at[8 + k], after)
        returned.wait()
        own = own + back[k]
        every.wait_recv()
        mine.wait()
        total = rs[k, 0]
        for n in range(1, DEV):
            total = total + rs[k, n]
        held = first_group * jnp.concatenate(
            [own[:, :half], own[:, half:], jnp.zeros((1, half), F32)], axis=0
        )
        total = total + held
        xs[k, g] = total
        stage[k] = total
        copies = [
            remote(
                stage.at[k], xs.at[k, g], sem_s.at[12 + n], sem_r.at[9 + n + 3 * k],
                {"grp": lax.rem(g + n, GRP), "dev": d},
            )
            for n in (2, 1, 3)
        ]
        for c in copies:
            c.start()
        every.wait_send()
        for c in copies:
            c.wait()
        total = (xs[k, 0] + xs[k, 1]) + (xs[k, 2] + xs[k, 3])
        column = jnp.concatenate([total[:fields], total[fields : 2 * fields]], axis=1)
        image = jnp.where(g == 0, column, own)
        return image, column, total[2 * fields :]

    ahead_obs.wait()
    mine_obs.wait()
    every_obs.wait_recv()
    b, prec = obs_v[...], noise_v[...]
    v0, w0, u0 = apply(b, prev_obs[...], all_obs)
    kept = prec * b
    image0, column, row = reduce(u0, w0 + kept, to_row([b * b, v0 * w0 + kept * b]), 0)
    rr0, p0 = from_row(row, 0, fields), from_row(row, 1, fields)
    alpha0 = rr0 / p0
    r1 = b - alpha0 * image0
    rcol[0] = r1
    rcol[1] = col_obs[...] - alpha0 * column
    ahead = remote(rcol.at[0], prev1, sem_s.at[11], sem_r.at[16], after)
    ahead.start()
    mine = local_copy(rcol.at[1], ag.at[d], 0)
    every = spread(rcol.at[1], ag, 12, 17)
    ahead.wait()
    mine.wait()
    every.wait()
    v1, w1, u1 = apply(r1, prev1[...], ag)
    kept = prec * r1
    image1, column, row = reduce(
        u1, w1 + kept, to_row([v1 * w1 + kept * r1, v1 * w0 + kept * b, r1 * r1]), 1
    )
    s1, s2, rr1 = (from_row(row, k, fields) for k in range(3))
    beta = rr1 / rr0
    alpha1 = rr1 / (s1 + 2.0 * beta * s2 + beta * beta * p0)
    image1 = image1 + beta * image0
    out[0] = alpha0 * b + alpha1 * (r1 + beta * b)
    out[1] = r1 - alpha1 * image1
    every_loc.wait_send()
    every_obs.wait_send()

    @pl.when(g == 0)
    def _():
        for c in column_loc + column_obs:
            c.wait_send()


def local(locations, neighbours, observations, noise_prec):
    points, fields = locations.shape[2], observations.shape[1]
    vmem = pl.BlockSpec(memory_space=pltpu.VMEM)
    hbm = pl.BlockSpec(memory_space=pltpu.HBM)

    def f32(*shape):
        return pltpu.VMEM(shape, F32)

    tall = 2 * fields + 1
    held = [
        pltpu.with_memory_space_constraint(x, pltpu.HBM)
        for x in (neighbours, jnp.transpose(locations, (1, 0, 2)), observations, noise_prec)
    ]
    both = pl.pallas_call(
        kernel,
        out_shape=jax.ShapeDtypeStruct((2, fields, points), F32),
        in_specs=[hbm] * 4,
        out_specs=vmem,
        scratch_shapes=[
            pltpu.SMEM((1, neighbours.shape[1]), jnp.int32),
            f32(3, 1, points), f32(fields, points), f32(fields, points),
            f32(3, 1, points), f32(fields, points),
            f32(3, 1, points), f32(fields, points),
            f32(DEV, 3, 1, points), f32(DEV, fields, points),
            f32(4, 4, points, points), f32(4, 3, points, points),
            f32(points, points), f32(points, points),
            pltpu.VMEM((2, points, 3 * points), BF16), pltpu.VMEM((2, points, points), BF16),
            f32(2, DEV, tall, points // 2), f32(2, DEV, tall, points // 2),
            f32(2, GRP, tall, points // 2), f32(2, tall, points // 2),
            f32(2, fields, points), f32(2, fields, points),
            f32(2, fields, points), f32(fields, points), f32(DEV, fields, points),
            pltpu.SemaphoreType.DMA((4,)),
            pltpu.SemaphoreType.DMA((4,)),
            pltpu.SemaphoreType.DMA((16,)),
            pltpu.SemaphoreType.DMA((18,)),
        ],
        compiler_params=pltpu.CompilerParams(
            collective_id=0, has_side_effects=True, vmem_limit_bytes=48 << 20
        ),
    )(*held)
    return both[:1], both[1:]


def solution(mesh):
    placed = (
        P(("grp", "dev"), None, None),
        P(("grp", "dev"), None),
        P(("grp", "dev"), None, None),
        P(("grp", "dev"), None, None),
    )
    return jax.shard_map(
        local,
        mesh=mesh,
        in_specs=placed,
        out_specs=(P(("grp", "dev"), None, None), P(("grp", "dev"), None, None)),
        check_vma=False,
    )
```

```python
import math

import jax
import jax.numpy as jnp
from jax import lax
from jax.experimental import pallas as pl
from jax.experimental.pallas import tpu as pltpu
from jax.sharding import PartitionSpec as P

SCALE_LENGTH = 0.5
NUGGET = 0.5
SQRT_THREE = math.sqrt(3.0)
F32 = jnp.float32
BF16 = jnp.bfloat16
NN = (((1,), (0,)), ((), ()))
NT = (((1,), (1,)), ((), ()))
DOUBLINGS, FULL = 7, 4
GRP, DEV = 4, 32


def coefficients(size):
    low, high = NUGGET, size + NUGGET
    tau = (high + low) / (high - low)
    rows = []
    for _ in range(DOUBLINGS):
        twice = 2.0 * tau * tau - 1.0
        rows.append((2.0 * tau * tau / twice, 1.0 / twice))
        tau = twice
    return rows, 2.0 / (high + low)


def pick(values, n):
    out = jnp.float32(values[-1])
    for k in range(len(values) - 2, -1, -1):
        out = jnp.where(n == k, jnp.float32(values[k]), out)
    return out


def split(x):
    high = x.astype(BF16)
    return high, (x - high.astype(F32)).astype(BF16)


def dot(a, b, dims=NN):
    return lax.dot_general(a, b, dims, preferred_element_type=F32)


def dot3(a, b, dims=NN):
    return dot(a[0], b[0], dims) + (dot(a[0], b[1], dims) + dot(a[1], b[0], dims))


def dot6(a, b, dims=NN):
    return lax.dot_general(
        a, b, dims, preferred_element_type=F32, precision=lax.Precision.HIGHEST
    )


def neighbourhood():
    g, d = lax.axis_index("grp"), lax.axis_index("dev")
    flat = g * DEV + d
    after, before = lax.rem(flat + 1, GRP * DEV), lax.rem(flat + GRP * DEV - 1, GRP * DEV)
    return g, d, place(after), place(before)


def mates(d):
    far = (2, 1, 3, 0)
    y, z, c = d // 8, lax.rem(d // 2, 4), lax.rem(d, 2)
    ys = {k: lax.rem(y + k, 4) * 8 for k in far}
    zs = {k: lax.rem(z + k, 4) * 2 for k in far}
    cs = {1: 1 - c, 0: c}
    return [ys[a] + (zs[b] + cs[e]) for a in far for b in far for e in (1, 0)][:-1]


def place(flat):
    return {"grp": flat // DEV, "dev": lax.rem(flat, DEV)}


def greet(g, d, after, before):
    barrier = pltpu.get_barrier_semaphore()

    def one(k, carry):
        pl.semaphore_signal(
            barrier, 1, device_id={"grp": g, "dev": lax.rem(d + k, DEV)}
        )
        return carry

    lax.fori_loop(1, DEV, one, 0)
    for k in range(1, GRP):
        pl.semaphore_signal(barrier, 1, device_id={"grp": lax.rem(g + k, GRP), "dev": d})
    pl.semaphore_signal(barrier, 1, device_id=after)
    pl.semaphore_signal(barrier, 1, device_id=before)
    return barrier


def remote(src, dst, send, recv, device):
    return pltpu.make_async_remote_copy(
        src_ref=src, dst_ref=dst, send_sem=send, recv_sem=recv, device_id=device
    )


def lane(shape):
    return lax.broadcasted_iota(jnp.int32, shape, 1)


def sublane(shape):
    return lax.broadcasted_iota(jnp.int32, shape, 0)


def to_row(parts):
    fields = parts[0].shape[0]
    spread = jnp.zeros((fields, 128), F32)
    slot = lane(spread.shape) - sublane(spread.shape)
    for k, part in enumerate(parts):
        spread = jnp.where(slot == k * fields, jnp.sum(part, axis=1, keepdims=True), spread)
    return jnp.sum(spread, axis=0, keepdims=True)


def from_row(row, k, fields):
    spread = jnp.broadcast_to(row, (fields, 128))
    slot = lane(spread.shape) - sublane(spread.shape)
    return jnp.sum(jnp.where(slot == k * fields, spread, 0.0), axis=1, keepdims=True)


def kernel(
    near_hbm, loc, obs, noise,
    out,
    near, loc_v, obs_v, noise_v, prev_loc, prev_obs, col_loc, col_obs, all_loc, all_obs,
    tiles, low, g_mat, p_mat,
    msg, rs, xs, stage, hop, back, rcol, prev1, ag,
    sem_in, sem_mine, sem_s, sem_r,
):
    fields, size = obs_v.shape
    g, d, after, before = neighbourhood()
    barrier = greet(g, d, after, before)
    incoming = [
        pltpu.make_async_copy(src, dst, sem_in.at[k])
        for k, (src, dst) in enumerate(
            ((loc, loc_v), (near_hbm, near), (obs.at[0], obs_v), (noise.at[0], noise_v))
        )
    ]
    for c in incoming:
        c.start()
    others = pl.ds(0, DEV - 1)
    plane = mates(d)
    eye = (sublane((size, size)) == lane((size, size))).astype(F32)
    rows, first = coefficients(size)
    first_group = jnp.where(g == 0, 1.0, 0.0).astype(F32)
    def points(value):
        flat = [value[c] for c in range(3)]
        upright = jnp.concatenate(flat + [jnp.zeros((5, size), F32)], axis=0).T
        return flat, upright

    def covariance(i, j):
        total = None
        for c in range(3):
            offset = pts[i][1][:, c : c + 1] - pts[j][0][c]
            total = offset * offset if total is None else total + offset * offset
        scaled = (SQRT_THREE / SCALE_LENGTH) * jnp.sqrt(total)
        value = (1.0 + scaled) * jnp.exp(-scaled) * (live[i] * live[j])
        if i == j:
            value = value + eye * (NUGGET * live[i] + (1.0 - live[i]))
        tiles[i, j] = value

    def spread(src, dst, s, r):
        for m in plane:
            remote(src, dst.at[d], sem_s.at[s], sem_r.at[r], {"grp": g, "dev": m}).start()
        piece = dst.at[others]
        return remote(piece, piece, sem_s.at[s], sem_r.at[r], after)

    def local_copy(src, dst, k):
        c = pltpu.make_async_copy(src, dst, sem_mine.at[k])
        c.start()
        return c

    incoming[0].wait()
    incoming[1].wait()
    wi, wj = near[0, 2], near[0, 3]
    live = [jnp.where(near[0, s] >= 0, 1.0, 0.0).astype(F32) for s in (0, 2, 3)] + [1.0]
    pts = [None, None, None, points(loc_v)]
    covariance(3, 3)
    pl.semaphore_wait(barrier, DEV - 1 + GRP - 1 + 2)
    ahead_loc = remote(loc_v, prev_loc, sem_s.at[0], sem_r.at[0], after)
    column_loc = [
        remote(loc_v, col_loc, sem_s.at[1 + k], sem_r.at[1], {"grp": k, "dev": d})
        for k in range(1, GRP)
    ]
    own_loc = pltpu.make_async_copy(loc_v, col_loc, sem_mine.at[0])

    @pl.when(g == 0)
    def _():
        for c in column_loc:
            c.start()
        own_loc.start()

    ahead_loc.start()
    incoming[2].wait()
    incoming[3].wait()
    ahead_obs = remote(obs_v, prev_obs, sem_s.at[5], sem_r.at[2], after)
    column_obs = [
        remote(obs_v, col_obs, sem_s.at[5 + k], sem_r.at[3], {"grp": k, "dev": d})
        for k in range(1, GRP)
    ]
    own_obs = pltpu.make_async_copy(obs_v, col_obs, sem_mine.at[1])
    ahead_obs.start()

    @pl.when(g == 0)
    def _():
        for c in column_obs:
            c.start()
        own_obs.start()

    ahead_loc.wait()
    pts[0] = points(prev_loc)
    covariance(0, 0)

    @pl.when(g == 0)
    def _():
        own_loc.wait()

    @pl.when(g != 0)
    def _():
        column_loc[0].wait_recv()

    mine_loc = local_copy(col_loc, all_loc.at[d], 2)
    every_loc = spread(col_loc, all_loc, 9, 4)

    def inverse(k, jobs=()):
        jobs = list(jobs)
        r = eye - first * tiles[k, k]
        x = (first * rows[0][0]) * (eye + r)
        pair = split(r)
        r = rows[0][0] * dot3(pair, pair) - rows[0][1] * eye
        for n, (a, c) in enumerate(rows[1:], 1):
            pair, halves = split(r), split(x)
            if n < FULL:
                moved, square = dot3(halves, pair), dot3(pair, pair)
            else:
                moved = dot(halves[0], pair[0]) + dot(halves[1], pair[0])
                square = dot(pair[0], pair[0])
            if jobs:
                jobs.pop(0)()
            x = a * (x + moved)
            r = a * square - c * eye
        left = eye - dot6(tiles[k, k], x)
        for job in jobs:
            job()
        halves, left = split(x), left.astype(BF16)
        return x + (dot(halves[0], left) + dot(halves[1], left))

    def lower(i, k, inv):
        low[i, k] = dot6(tiles[i, k], inv)

    def update(i, j, k):
        tiles[i, j] = tiles[i, j] - dot6(low[i, k], tiles[j, k], NT)

    def put(k, value):
        high, rest = split(value)
        g_mat[0, :, k * size : (k + 1) * size] = high
        g_mat[1, :, k * size : (k + 1) * size] = rest

    inv = inverse(0)
    covariance(3, 0)
    low[3, 0] = dot6(tiles[3, 0], inv)
    tiles[3, 3] = tiles[3, 3] - dot6(low[3, 0], tiles[3, 0], NT)

    @pl.when(g == 0)
    def _():
        own_obs.wait()

    @pl.when(g != 0)
    def _():
        column_obs[0].wait_recv()

    mine_loc.wait()
    every_loc.wait_recv()
    mine_obs = local_copy(col_obs, all_obs.at[d], 3)
    every_obs = spread(col_obs, all_obs, 10, 5)
    pts[1] = points(all_loc[jnp.maximum(wi, 0)])
    pts[2] = points(all_loc[jnp.maximum(wj, 0)])
    covariance(1, 0)
    covariance(1, 1)
    lower(1, 0, inv)
    update(1, 1, 0)

    def one():
        covariance(2, 0)
        lower(2, 0, inv)

    def two():
        covariance(2, 1)
        update(2, 1, 0)

    def three():
        covariance(2, 2)
        update(2, 2, 0)

    def four():
        covariance(3, 1)
        update(3, 1, 0)

    def five():
        covariance(3, 2)
        update(3, 2, 0)

    inv1 = inverse(1, (one, two, three, four, five))
    lower(2, 1, inv1)
    update(2, 2, 1)

    def six():
        lower(3, 1, inv1)

    def seven():
        update(3, 2, 1)

    def eight():
        update(3, 3, 1)

    def nine():
        low[2, 0] = dot6(low[2, 1], low[1, 0]) - low[2, 0]

    def ten():
        low[3, 0] = dot6(low[3, 1], low[1, 0]) - low[3, 0]

    inv2 = inverse(2, (six, seven, eight, nine, ten))
    lower(3, 2, inv2)
    update(3, 3, 2)

    def eleven():
        put(2, -low[3, 2])

    def twelve():
        put(1, dot6(low[3, 2], low[2, 1]) - low[3, 1])

    def thirteen():
        put(0, low[3, 0] - dot6(low[3, 2], low[2, 0]))

    inv3 = inverse(3, (eleven, twelve, thirteen))
    p_mat[0], p_mat[1] = split(inv3)

    def dot_small(rows, mat, dims):
        high, rest = split(rows)
        return dot(high, mat[0], dims) + (dot(high, mat[1], dims) + dot(rest, mat[0], dims))

    def apply(own, before_rows, table):
        slots = jnp.concatenate(
            [before_rows, table[jnp.maximum(wi, 0)], table[jnp.maximum(wj, 0)]], axis=1
        )
        v = own + dot_small(slots, g_mat, NT)
        w = dot_small(v, p_mat, NN)
        return v, w, dot_small(w, g_mat, NN)

    def reduce(u, own, row, k):
        hop[k] = u[:, :size]
        half = size // 2
        ui, uj = u[:, size : 2 * size], u[:, 2 * size :]

        def fill(m, carry):
            fi = jnp.where(wi == m, 1.0, 0.0).astype(F32)
            fj = jnp.where(wj == m, 1.0, 0.0).astype(F32)
            block = fi * ui + fj * uj
            msg[k, m, :fields] = block[:, :half]
            msg[k, m, fields : 2 * fields] = block[:, half:]
            msg[k, m, 2 * fields :] = row
            return carry

        lax.fori_loop(0, DEV, fill, 0)
        returned = remote(hop.at[k], back.at[k], sem_s.at[11], sem_r.at[6 + k], before)
        returned.start()
        mine = local_copy(msg.at[k, d], rs.at[k, d], 0)

        for m in plane:
            remote(
                msg.at[k, m], rs.at[k, d], sem_s.at[12], sem_r.at[8 + k], {"grp": g, "dev": m}
            ).start()
        piece = rs.at[k, others]
        every = remote(piece, piece, sem_s.at[12], sem_r.at[8 + k], after)
        returned.wait()
        own = own + back[k]
        every.wait_recv()
        mine.wait()
        total = rs[k, 0]
        for n in range(1, DEV):
            total = total + rs[k, n]
        held = first_group * jnp.concatenate(
            [own[:, :half], own[:, half:], jnp.zeros((1, half), F32)], axis=0
        )
        total = total + held
        xs[k, g] = total
        stage[k] = total
        copies = [
            remote(
                stage.at[k], xs.at[k, g], sem_s.at[12 + n], sem_r.at[9 + n + 3 * k],
                {"grp": lax.rem(g + n, GRP), "dev": d},
            )
            for n in (2, 1, 3)
        ]
        for c in copies:
            c.start()
        every.wait_send()
        for c in copies:
            c.wait()
        total = (xs[k, 0] + xs[k, 1]) + (xs[k, 2] + xs[k, 3])
        column = jnp.concatenate([total[:fields], total[fields : 2 * fields]], axis=1)
        image = jnp.where(g == 0, column, own)
        return image, column, total[2 * fields :]

    ahead_obs.wait()
    mine_obs.wait()
    every_obs.wait_recv()
    b, prec = obs_v[...], noise_v[...]
    v0, w0, u0 = apply(b, prev_obs[...], all_obs)
    kept = prec * b
    image0, column, row = reduce(u0, w0 + kept, to_row([b * b, v0 * w0 + kept * b]), 0)
    rr0, p0 = from_row(row, 0, fields), from_row(row, 1, fields)
    alpha0 = rr0 / p0
    r1 = b - alpha0 * image0
    rcol[0] = r1
    rcol[1] = col_obs[...] - alpha0 * column
    ahead = remote(rcol.at[0], prev1, sem_s.at[11], sem_r.at[16], after)
    ahead.start()
    mine = local_copy(rcol.at[1], ag.at[d], 0)
    every = spread(rcol.at[1], ag, 12, 17)
    ahead.wait()
    mine.wait()
    every.wait()
    v1, w1, u1 = apply(r1, prev1[...], ag)
    kept = prec * r1
    image1, column, row = reduce(
        u1, w1 + kept, to_row([v1 * w1 + kept * r1, v1 * w0 + kept * b, r1 * r1]), 1
    )
    s1, s2, rr1 = (from_row(row, k, fields) for k in range(3))
    beta = rr1 / rr0
    alpha1 = rr1 / (s1 + 2.0 * beta * s2 + beta * beta * p0)
    image1 = image1 + beta * image0
    out[0] = alpha0 * b + alpha1 * (r1 + beta * b)
    out[1] = r1 - alpha1 * image1
    every_loc.wait_send()
    every_obs.wait_send()

    @pl.when(g == 0)
    def _():
        for c in column_loc + column_obs:
            c.wait_send()


def local(locations, neighbours, observations, noise_prec):
    points, fields = locations.shape[2], observations.shape[1]
    vmem = pl.BlockSpec(memory_space=pltpu.VMEM)
    hbm = pl.BlockSpec(memory_space=pltpu.HBM)

    def f32(*shape):
        return pltpu.VMEM(shape, F32)

    tall = 2 * fields + 1
    held = [
        pltpu.with_memory_space_constraint(x, pltpu.HBM)
        for x in (neighbours, jnp.transpose(locations, (1, 0, 2)), observations, noise_prec)
    ]
    both = pl.pallas_call(
        kernel,
        out_shape=jax.ShapeDtypeStruct((2, fields, points), F32),
        in_specs=[hbm] * 4,
        out_specs=vmem,
        scratch_shapes=[
            pltpu.SMEM((1, neighbours.shape[1]), jnp.int32),
            f32(3, 1, points), f32(fields, points), f32(fields, points),
            f32(3, 1, points), f32(fields, points),
            f32(3, 1, points), f32(fields, points),
            f32(DEV, 3, 1, points), f32(DEV, fields, points),
            f32(4, 4, points, points), f32(4, 3, points, points),
            pltpu.VMEM((2, points, 3 * points), BF16), pltpu.VMEM((2, points, points), BF16),
            f32(2, DEV, tall, points // 2), f32(2, DEV, tall, points // 2),
            f32(2, GRP, tall, points // 2), f32(2, tall, points // 2),
            f32(2, fields, points), f32(2, fields, points),
            f32(2, fields, points), f32(fields, points), f32(DEV, fields, points),
            pltpu.SemaphoreType.DMA((4,)),
            pltpu.SemaphoreType.DMA((4,)),
            pltpu.SemaphoreType.DMA((16,)),
            pltpu.SemaphoreType.DMA((18,)),
        ],
        compiler_params=pltpu.CompilerParams(
            collective_id=0, has_side_effects=True, vmem_limit_bytes=48 << 20
        ),
    )(*held)
    return both[:1], both[1:]


def solution(mesh):
    placed = (
        P(("grp", "dev"), None, None),
        P(("grp", "dev"), None),
        P(("grp", "dev"), None, None),
        P(("grp", "dev"), None, None),
    )
    return jax.shard_map(
        local,
        mesh=mesh,
        in_specs=placed,
        out_specs=(P(("grp", "dev"), None, None), P(("grp", "dev"), None, None)),
        check_vma=False,
    )
```

```python
import math

import jax
import jax.numpy as jnp
from jax import lax
from jax.experimental import pallas as pl
from jax.experimental.pallas import tpu as pltpu
from jax.sharding import PartitionSpec as P

SCALE_LENGTH = 0.5
NUGGET = 0.5
SQRT_THREE = math.sqrt(3.0)
F32 = jnp.float32
BF16 = jnp.bfloat16
NN = (((1,), (0,)), ((), ()))
NT = (((1,), (1,)), ((), ()))
DOUBLINGS, FULL, LEAD = 7, 4, 6
GRP, DEV = 4, 32


def coefficients(size):
    low, high = NUGGET, size + NUGGET
    tau = (high + low) / (high - low)
    rows = []
    for _ in range(DOUBLINGS):
        twice = 2.0 * tau * tau - 1.0
        rows.append((2.0 * tau * tau / twice, 1.0 / twice))
        tau = twice
    return rows, 2.0 / (high + low)


def pick(values, n):
    out = jnp.float32(values[-1])
    for k in range(len(values) - 2, -1, -1):
        out = jnp.where(n == k, jnp.float32(values[k]), out)
    return out


def split(x):
    high = x.astype(BF16)
    return high, (x - high.astype(F32)).astype(BF16)


def dot(a, b, dims=NN):
    return lax.dot_general(a, b, dims, preferred_element_type=F32)


def dot3(a, b, dims=NN):
    return dot(a[0], b[0], dims) + (dot(a[0], b[1], dims) + dot(a[1], b[0], dims))


def dot6(a, b, dims=NN):
    return lax.dot_general(
        a, b, dims, preferred_element_type=F32, precision=lax.Precision.HIGHEST
    )


def neighbourhood():
    g, d = lax.axis_index("grp"), lax.axis_index("dev")
    flat = g * DEV + d
    after, before = lax.rem(flat + 1, GRP * DEV), lax.rem(flat + GRP * DEV - 1, GRP * DEV)
    return g, d, place(after), place(before)


def mates(d):
    far = (2, 1, 3, 0)
    y, z, c = d // 8, lax.rem(d // 2, 4), lax.rem(d, 2)
    ys = {k: lax.rem(y + k, 4) * 8 for k in far}
    zs = {k: lax.rem(z + k, 4) * 2 for k in far}
    cs = {1: 1 - c, 0: c}
    return [ys[a] + (zs[b] + cs[e]) for a in far for b in far for e in (1, 0)][:-1]


def place(flat):
    return {"grp": flat // DEV, "dev": lax.rem(flat, DEV)}


def greet(g, d, plane, after, before):
    barrier = pltpu.get_barrier_semaphore()
    for k in (2, 1, 3):
        pl.semaphore_signal(barrier, 1, device_id={"grp": lax.rem(g + k, GRP), "dev": d})
    pl.semaphore_signal(barrier, 1, device_id=before)
    pl.semaphore_signal(barrier, 1, device_id=after)
    for m in plane:
        pl.semaphore_signal(barrier, 1, device_id={"grp": g, "dev": m})
    return barrier


def remote(src, dst, send, recv, device):
    return pltpu.make_async_remote_copy(
        src_ref=src, dst_ref=dst, send_sem=send, recv_sem=recv, device_id=device
    )


def lane(shape):
    return lax.broadcasted_iota(jnp.int32, shape, 1)


def sublane(shape):
    return lax.broadcasted_iota(jnp.int32, shape, 0)


def to_row(parts):
    fields = parts[0].shape[0]
    spread = jnp.zeros((fields, 128), F32)
    slot = lane(spread.shape) - sublane(spread.shape)
    for k, part in enumerate(parts):
        spread = jnp.where(slot == k * fields, jnp.sum(part, axis=1, keepdims=True), spread)
    return jnp.sum(spread, axis=0, keepdims=True)


def from_row(row, k, fields):
    spread = jnp.broadcast_to(row, (fields, 128))
    slot = lane(spread.shape) - sublane(spread.shape)
    return jnp.sum(jnp.where(slot == k * fields, spread, 0.0), axis=1, keepdims=True)


def kernel(
    near_hbm, loc, obs, noise,
    out,
    near, loc_v, obs_v, noise_v, prev_loc, prev_obs, col_loc, col_obs, all_loc, all_obs,
    tiles, low, g_mat, p_mat, h_mat, pre,
    msg, rs, xs, stage, hop, back, rcol, prev1, ag,
    sem_in, sem_mine, sem_s, sem_r,
):
    fields, size = obs_v.shape
    g, d, after, before = neighbourhood()
    plane = mates(d)
    barrier = greet(g, d, plane, after, before)
    incoming = [
        pltpu.make_async_copy(src, dst, sem_in.at[k])
        for k, (src, dst) in enumerate(
            ((loc, loc_v), (near_hbm, near), (obs.at[0], obs_v), (noise.at[0], noise_v))
        )
    ]
    for c in incoming:
        c.start()
    others = pl.ds(0, DEV - 1)
    eye = (sublane((size, size)) == lane((size, size))).astype(F32)
    rows, first = coefficients(size)
    first_group = jnp.where(g == 0, 1.0, 0.0).astype(F32)
    def points(value):
        flat = [value[c] for c in range(3)]
        upright = jnp.concatenate(flat + [jnp.zeros((5, size), F32)], axis=0).T
        return flat, upright

    def covariance(i, j):
        total = None
        for c in range(3):
            offset = pts[i][1][:, c : c + 1] - pts[j][0][c]
            total = offset * offset if total is None else total + offset * offset
        scaled = (SQRT_THREE / SCALE_LENGTH) * jnp.sqrt(total)
        value = (1.0 + scaled) * jnp.exp(-scaled) * (live[i] * live[j])
        if i == j:
            value = value + eye * (NUGGET * live[i] + (1.0 - live[i]))
        tiles[i, j] = value

    def spread(src, dst, s, r):
        for m in plane:
            remote(src, dst.at[d], sem_s.at[s], sem_r.at[r], {"grp": g, "dev": m}).start()
        piece = dst.at[others]
        return remote(piece, piece, sem_s.at[s], sem_r.at[r], after)

    def local_copy(src, dst, k):
        c = pltpu.make_async_copy(src, dst, sem_mine.at[k])
        c.start()
        return c

    incoming[0].wait()
    incoming[1].wait()
    wi, wj = near[0, 2], near[0, 3]
    live = [jnp.where(near[0, s] >= 0, 1.0, 0.0).astype(F32) for s in (0, 2, 3)] + [1.0]
    pts = [None, None, None, points(loc_v)]
    covariance(3, 3)
    pl.semaphore_wait(barrier, DEV - 1 + GRP - 1 + 2)
    ahead_loc = remote(loc_v, prev_loc, sem_s.at[0], sem_r.at[0], after)
    column_loc = [
        remote(loc_v, col_loc, sem_s.at[1 + k], sem_r.at[1], {"grp": k, "dev": d})
        for k in range(1, GRP)
    ]
    own_loc = pltpu.make_async_copy(loc_v, col_loc, sem_mine.at[0])

    @pl.when(g == 0)
    def _():
        for c in column_loc:
            c.start()
        own_loc.start()

    ahead_loc.start()
    incoming[2].wait()
    incoming[3].wait()
    ahead_obs = remote(obs_v, prev_obs, sem_s.at[5], sem_r.at[2], after)
    column_obs = [
        remote(obs_v, col_obs, sem_s.at[5 + k], sem_r.at[3], {"grp": k, "dev": d})
        for k in range(1, GRP)
    ]
    own_obs = pltpu.make_async_copy(obs_v, col_obs, sem_mine.at[1])
    ahead_obs.start()

    @pl.when(g == 0)
    def _():
        for c in column_obs:
            c.start()
        own_obs.start()

    ahead_loc.wait()
    pts[0] = points(prev_loc)
    covariance(0, 0)

    @pl.when(g == 0)
    def _():
        own_loc.wait()

    @pl.when(g != 0)
    def _():
        column_loc[0].wait_recv()

    mine_loc = local_copy(col_loc, all_loc.at[d], 2)
    every_loc = spread(col_loc, all_loc, 9, 4)

    def inverse(k, jobs=()):
        jobs = list(jobs)
        r = eye - first * tiles[k, k]
        x = (first * rows[0][0]) * (eye + r)
        pair = split(r)
        r = rows[0][0] * dot3(pair, pair) - rows[0][1] * eye
        for n, (a, c) in enumerate(rows[1:], 1):
            pair, halves = split(r), split(x)
            if n < FULL:
                moved, square = dot3(halves, pair), dot3(pair, pair)
            else:
                moved = dot(halves[0], pair[0]) + dot(halves[1], pair[0])
                square = dot(pair[0], pair[0])
            if jobs:
                jobs.pop(0)()
            x = a * (x + moved)
            r = a * square - c * eye
        left = eye - dot6(tiles[k, k], x)
        for job in jobs:
            job()
        halves, left = split(x), left.astype(BF16)
        return x + (dot(halves[0], left) + dot(halves[1], left))

    def lower(i, k, inv):
        low[i, k] = dot6(tiles[i, k], inv)

    def update(i, j, k):
        tiles[i, j] = tiles[i, j] - dot6(low[i, k], tiles[j, k], NT)

    def put(k, value):
        high, rest = split(value)
        g_mat[0, :, k * size : (k + 1) * size] = high
        g_mat[1, :, k * size : (k + 1) * size] = rest

    inv = inverse(0)
    covariance(3, 0)
    low[3, 0] = dot6(tiles[3, 0], inv)
    tiles[3, 3] = tiles[3, 3] - dot6(low[3, 0], tiles[3, 0], NT)

    @pl.when(g == 0)
    def _():
        own_obs.wait()

    @pl.when(g != 0)
    def _():
        column_obs[0].wait_recv()

    mine_loc.wait()
    every_loc.wait_recv()
    mine_obs = local_copy(col_obs, all_obs.at[d], 3)
    every_obs = spread(col_obs, all_obs, 10, 5)
    pts[1] = points(all_loc[jnp.maximum(wi, 0)])
    pts[2] = points(all_loc[jnp.maximum(wj, 0)])
    covariance(1, 0)
    covariance(1, 1)
    lower(1, 0, inv)
    update(1, 1, 0)

    def one():
        covariance(2, 0)
        lower(2, 0, inv)

    def two():
        covariance(2, 1)
        update(2, 1, 0)

    def three():
        covariance(2, 2)
        update(2, 2, 0)

    def four():
        covariance(3, 1)
        update(3, 1, 0)

    def five():
        covariance(3, 2)
        update(3, 2, 0)

    inv1 = inverse(1, (one, two, three, four, five))
    lower(2, 1, inv1)
    update(2, 2, 1)

    def six():
        lower(3, 1, inv1)

    def seven():
        update(3, 2, 1)

    def eight():
        update(3, 3, 1)

    def nine():
        low[2, 0] = dot6(low[2, 1], low[1, 0]) - low[2, 0]

    def ten():
        low[3, 0] = dot6(low[3, 1], low[1, 0]) - low[3, 0]

    inv2 = inverse(2, (six, seven, eight, nine, ten))
    lower(3, 2, inv2)
    update(3, 3, 2)

    def eleven():
        put(2, -low[3, 2])

    def twelve():
        put(1, dot6(low[3, 2], low[2, 1]) - low[3, 1])

    def thirteen():
        put(0, low[3, 0] - dot6(low[3, 2], low[2, 0]))

    def dot_small(rows, mat, dims):
        high, rest = split(rows)
        return dot(high, mat[0], dims) + (dot(high, mat[1], dims) + dot(rest, mat[0], dims))

    def forward(own, before_rows, table):
        slots = jnp.concatenate(
            [before_rows, table[jnp.maximum(wi, 0)], table[jnp.maximum(wj, 0)]], axis=1
        )
        return own + dot_small(slots, g_mat, NT)

    def fourteen():
        pre[...] = forward(obs_v[...], prev_obs[...], all_obs)

    ahead_obs.wait()
    mine_obs.wait()
    every_obs.wait_recv()
    inv3 = inverse(3, (eleven, twelve, thirteen, fourteen))
    p_mat[0], p_mat[1] = split(inv3)

    def reduce(u, own, row, k, filler):
        hop[k] = u[:, :size]
        half = size // 2
        ui, uj = u[:, size : 2 * size], u[:, 2 * size :]

        def fill(m):
            fi = jnp.where(wi == m, 1.0, 0.0).astype(F32)
            fj = jnp.where(wj == m, 1.0, 0.0).astype(F32)
            block = fi * ui + fj * uj
            msg[k, m, :fields] = block[:, :half]
            msg[k, m, fields : 2 * fields] = block[:, half:]
            msg[k, m, 2 * fields :] = row

        returned = remote(hop.at[k], back.at[k], sem_s.at[11], sem_r.at[6 + k], before)
        targets = plane + [d]
        for m in targets[:LEAD]:
            fill(m)
        returned.start()
        for n, m in enumerate(plane):
            if n + LEAD < DEV:
                fill(targets[n + LEAD])
            remote(
                msg.at[k, m], rs.at[k, d], sem_s.at[12], sem_r.at[8 + k], {"grp": g, "dev": m}
            ).start()
        mine = local_copy(msg.at[k, d], rs.at[k, d], 0)
        filler()
        piece = rs.at[k, others]
        every = remote(piece, piece, sem_s.at[12], sem_r.at[8 + k], after)
        returned.wait()
        own = own + back[k]
        every.wait_recv()
        mine.wait()
        sums = [rs[k, n] for n in range(4)]
        for n in range(4, DEV):
            sums[n % 4] = sums[n % 4] + rs[k, n]
        total = (sums[0] + sums[1]) + (sums[2] + sums[3])
        held = first_group * jnp.concatenate(
            [own[:, :half], own[:, half:], jnp.zeros((1, half), F32)], axis=0
        )
        total = total + held
        xs[k, g] = total
        stage[k] = total
        copies = [
            remote(
                stage.at[k], xs.at[k, g], sem_s.at[12 + n], sem_r.at[9 + n + 3 * k],
                {"grp": lax.rem(g + n, GRP), "dev": d},
            )
            for n in (2, 1, 3)
        ]
        for c in copies:
            c.start()
        every.wait_send()
        for c in copies:
            c.wait()
        total = (xs[k, 0] + xs[k, 1]) + (xs[k, 2] + xs[k, 3])
        column = jnp.concatenate([total[:fields], total[fields : 2 * fields]], axis=1)
        image = jnp.where(g == 0, column, own)
        return image, column, total[2 * fields :]

    b, prec = obs_v[...], noise_v[...]
    v0 = pre[...]
    w0 = dot_small(v0, p_mat, NN)
    u0 = dot_small(w0, g_mat, NN)
    kept = prec * b

    def joined():
        left = (p_mat[0], p_mat[1])
        for k in range(3):
            cut = slice(k * size, (k + 1) * size)
            h_mat[0, :, cut], h_mat[1, :, cut] = split(
                dot3(left, (g_mat[0, :, cut], g_mat[1, :, cut]))
            )

    image0, column, row = reduce(u0, w0 + kept, to_row([b * b, v0 * w0 + kept * b]), 0, joined)
    rr0, p0 = from_row(row, 0, fields), from_row(row, 1, fields)
    alpha0 = rr0 / p0
    r1 = b - alpha0 * image0
    rcol[0] = r1
    rcol[1] = col_obs[...] - alpha0 * column
    ahead = remote(rcol.at[0], prev1, sem_s.at[11], sem_r.at[16], after)
    ahead.start()
    mine = local_copy(rcol.at[1], ag.at[d], 0)
    every = spread(rcol.at[1], ag, 12, 17)
    ahead.wait()
    mine.wait()
    every.wait()
    v1 = forward(r1, prev1[...], ag)
    w1 = dot_small(v1, p_mat, NN)
    u1 = dot_small(v1, h_mat, NN)
    kept = prec * r1
    image1, column, row = reduce(
        u1, w1 + kept, to_row([v1 * w1 + kept * r1, v1 * w0 + kept * b, r1 * r1]), 1,
        lambda: None,
    )
    s1, s2, rr1 = (from_row(row, k, fields) for k in range(3))
    beta = rr1 / rr0
    alpha1 = rr1 / (s1 + 2.0 * beta * s2 + beta * beta * p0)
    image1 = image1 + beta * image0
    out[0] = alpha0 * b + alpha1 * (r1 + beta * b)
    out[1] = r1 - alpha1 * image1
    every_loc.wait_send()
    every_obs.wait_send()

    @pl.when(g == 0)
    def _():
        for c in column_loc + column_obs:
            c.wait_send()


def local(locations, neighbours, observations, noise_prec):
    points, fields = locations.shape[2], observations.shape[1]
    vmem = pl.BlockSpec(memory_space=pltpu.VMEM)
    hbm = pl.BlockSpec(memory_space=pltpu.HBM)

    def f32(*shape):
        return pltpu.VMEM(shape, F32)

    tall = 2 * fields + 1
    held = [
        pltpu.with_memory_space_constraint(x, pltpu.HBM)
        for x in (neighbours, jnp.transpose(locations, (1, 0, 2)), observations, noise_prec)
    ]
    both = pl.pallas_call(
        kernel,
        out_shape=jax.ShapeDtypeStruct((2, fields, points), F32),
        in_specs=[hbm] * 4,
        out_specs=vmem,
        scratch_shapes=[
            pltpu.SMEM((1, neighbours.shape[1]), jnp.int32),
            f32(3, 1, points), f32(fields, points), f32(fields, points),
            f32(3, 1, points), f32(fields, points),
            f32(3, 1, points), f32(fields, points),
            f32(DEV, 3, 1, points), f32(DEV, fields, points),
            f32(4, 4, points, points), f32(4, 3, points, points),
            pltpu.VMEM((2, points, 3 * points), BF16), pltpu.VMEM((2, points, points), BF16),
            pltpu.VMEM((2, points, 3 * points), BF16), f32(fields, points),
            f32(2, DEV, tall, points // 2), f32(2, DEV, tall, points // 2),
            f32(2, GRP, tall, points // 2), f32(2, tall, points // 2),
            f32(2, fields, points), f32(2, fields, points),
            f32(2, fields, points), f32(fields, points), f32(DEV, fields, points),
            pltpu.SemaphoreType.DMA((4,)),
            pltpu.SemaphoreType.DMA((4,)),
            pltpu.SemaphoreType.DMA((16,)),
            pltpu.SemaphoreType.DMA((18,)),
        ],
        compiler_params=pltpu.CompilerParams(
            collective_id=0, has_side_effects=True, vmem_limit_bytes=48 << 20
        ),
    )(*held)
    return both[:1], both[1:]


def solution(mesh):
    placed = (
        P(("grp", "dev"), None, None),
        P(("grp", "dev"), None),
        P(("grp", "dev"), None, None),
        P(("grp", "dev"), None, None),
    )
    return jax.shard_map(
        local,
        mesh=mesh,
        in_specs=placed,
        out_specs=(P(("grp", "dev"), None, None), P(("grp", "dev"), None, None)),
        check_vma=False,
    )
```

```python
import math

import jax
import jax.numpy as jnp
from jax import lax
from jax.experimental import pallas as pl
from jax.experimental.pallas import tpu as pltpu
from jax.sharding import PartitionSpec as P

SCALE_LENGTH = 0.5
NUGGET = 0.5
SQRT_THREE = math.sqrt(3.0)
F32 = jnp.float32
BF16 = jnp.bfloat16
NN = (((1,), (0,)), ((), ()))
NT = (((1,), (1,)), ((), ()))
DOUBLINGS, FULL, LEAD = 7, 4, 6
GRP, DEV = 4, 32


def coefficients(size):
    low, high = NUGGET, size + NUGGET
    tau = (high + low) / (high - low)
    rows = []
    for _ in range(DOUBLINGS):
        twice = 2.0 * tau * tau - 1.0
        rows.append((2.0 * tau * tau / twice, 1.0 / twice))
        tau = twice
    return rows, 2.0 / (high + low)


def pick(values, n):
    out = jnp.float32(values[-1])
    for k in range(len(values) - 2, -1, -1):
        out = jnp.where(n == k, jnp.float32(values[k]), out)
    return out


def split(x):
    high = x.astype(BF16)
    return high, (x - high.astype(F32)).astype(BF16)


def dot(a, b, dims=NN):
    return lax.dot_general(a, b, dims, preferred_element_type=F32)


def dot3(a, b, dims=NN):
    return dot(a[0], b[0], dims) + (dot(a[0], b[1], dims) + dot(a[1], b[0], dims))


def dot6(a, b, dims=NN):
    return lax.dot_general(
        a, b, dims, preferred_element_type=F32, precision=lax.Precision.HIGHEST
    )


def neighbourhood():
    g, d = lax.axis_index("grp"), lax.axis_index("dev")
    flat = g * DEV + d
    after, before = lax.rem(flat + 1, GRP * DEV), lax.rem(flat + GRP * DEV - 1, GRP * DEV)
    return g, d, place(after), place(before)


def mates(d):
    far = (2, 1, 3, 0)
    y, z, c = d // 8, lax.rem(d // 2, 4), lax.rem(d, 2)
    ys = {k: lax.rem(y + k, 4) * 8 for k in far}
    zs = {k: lax.rem(z + k, 4) * 2 for k in far}
    cs = {1: 1 - c, 0: c}
    return [ys[a] + (zs[b] + cs[e]) for a in far for b in far for e in (1, 0)][:-1]


def place(flat):
    return {"grp": flat // DEV, "dev": lax.rem(flat, DEV)}


def greet(g, d, plane, after, before):
    barrier = pltpu.get_barrier_semaphore()
    for k in (2, 1, 3):
        pl.semaphore_signal(barrier, 1, device_id={"grp": lax.rem(g + k, GRP), "dev": d})
    pl.semaphore_signal(barrier, 1, device_id=before)
    pl.semaphore_signal(barrier, 1, device_id=after)
    for m in plane:
        pl.semaphore_signal(barrier, 1, device_id={"grp": g, "dev": m})
    return barrier


def remote(src, dst, send, recv, device):
    return pltpu.make_async_remote_copy(
        src_ref=src, dst_ref=dst, send_sem=send, recv_sem=recv, device_id=device
    )


def lane(shape):
    return lax.broadcasted_iota(jnp.int32, shape, 1)


def sublane(shape):
    return lax.broadcasted_iota(jnp.int32, shape, 0)


def to_row(parts):
    fields = parts[0].shape[0]
    spread = jnp.zeros((fields, 128), F32)
    slot = lane(spread.shape) - sublane(spread.shape)
    for k, part in enumerate(parts):
        spread = jnp.where(slot == k * fields, jnp.sum(part, axis=1, keepdims=True), spread)
    return jnp.sum(spread, axis=0, keepdims=True)


def from_row(row, k, fields):
    spread = jnp.broadcast_to(row, (fields, 128))
    slot = lane(spread.shape) - sublane(spread.shape)
    return jnp.sum(jnp.where(slot == k * fields, spread, 0.0), axis=1, keepdims=True)


def kernel(
    near_hbm, loc, obs, noise,
    out,
    near, loc_v, obs_v, noise_v, prev_loc, prev_obs, col_loc, col_obs, all_loc, all_obs,
    tiles, low, g_mat, p_mat, h_mat, pre,
    msg, rs, xs, stage, hop, back, rcol, prev1, ag,
    sem_in, sem_mine, sem_s, sem_r,
):
    fields, size = obs_v.shape
    g, d, after, before = neighbourhood()
    plane = mates(d)
    barrier = greet(g, d, plane, after, before)
    incoming = [
        pltpu.make_async_copy(src, dst, sem_in.at[k])
        for k, (src, dst) in enumerate(
            ((loc, loc_v), (near_hbm, near), (obs.at[0], obs_v), (noise.at[0], noise_v))
        )
    ]
    for c in incoming:
        c.start()
    others = pl.ds(0, DEV - 1)
    eye = (sublane((size, size)) == lane((size, size))).astype(F32)
    rows, first = coefficients(size)
    first_group = jnp.where(g == 0, 1.0, 0.0).astype(F32)
    def points(value):
        flat = [value[c] for c in range(3)]
        upright = jnp.concatenate(flat + [jnp.zeros((5, size), F32)], axis=0).T
        return flat, upright

    def covariance(i, j):
        total = None
        for c in range(3):
            offset = pts[i][1][:, c : c + 1] - pts[j][0][c]
            total = offset * offset if total is None else total + offset * offset
        scaled = (SQRT_THREE / SCALE_LENGTH) * jnp.sqrt(total)
        value = (1.0 + scaled) * jnp.exp(-scaled) * (live[i] * live[j])
        if i == j:
            value = value + eye * (NUGGET * live[i] + (1.0 - live[i]))
        tiles[i, j] = value

    def spread(src, dst, s, r):
        for m in plane:
            remote(src, dst.at[d], sem_s.at[s], sem_r.at[r], {"grp": g, "dev": m}).start()
        piece = dst.at[others]
        return remote(piece, piece, sem_s.at[s], sem_r.at[r], after)

    def local_copy(src, dst, k):
        c = pltpu.make_async_copy(src, dst, sem_mine.at[k])
        c.start()
        return c

    pl.semaphore_wait(barrier, DEV - 1 + GRP - 1 + 2)
    ahead_loc = remote(loc, prev_loc, sem_s.at[0], sem_r.at[0], after)
    column_loc = [
        remote(loc, col_loc, sem_s.at[1 + k], sem_r.at[1], {"grp": k, "dev": d})
        for k in range(1, GRP)
    ]
    own_loc = pltpu.make_async_copy(loc, col_loc, sem_mine.at[0])
    ahead_obs = remote(obs.at[0], prev_obs, sem_s.at[5], sem_r.at[2], after)
    column_obs = [
        remote(obs.at[0], col_obs, sem_s.at[5 + k], sem_r.at[3], {"grp": k, "dev": d})
        for k in range(1, GRP)
    ]
    own_obs = pltpu.make_async_copy(obs.at[0], col_obs, sem_mine.at[1])

    @pl.when(g == 0)
    def _():
        column_loc[1].start()
        column_loc[0].start()
        column_loc[2].start()
        own_loc.start()

    ahead_loc.start()
    incoming[0].wait()
    incoming[1].wait()
    wi, wj = near[0, 2], near[0, 3]
    live = [jnp.where(near[0, s] >= 0, 1.0, 0.0).astype(F32) for s in (0, 2, 3)] + [1.0]
    pts = [None, None, None, points(loc_v)]
    covariance(3, 3)
    incoming[2].wait()
    incoming[3].wait()

    @pl.when(g == 0)
    def _():
        own_loc.wait()

    @pl.when(g != 0)
    def _():
        column_loc[0].wait_recv()

    mine_loc = local_copy(col_loc, all_loc.at[d], 2)
    every_loc = spread(col_loc, all_loc, 9, 4)
    ahead_obs.start()

    @pl.when(g == 0)
    def _():
        for c in column_obs:
            c.start()
        own_obs.start()

    ahead_loc.wait()
    pts[0] = points(prev_loc)
    covariance(0, 0)
    def inverse(k, jobs=()):
        jobs = list(jobs)
        r = eye - first * tiles[k, k]
        x = (first * rows[0][0]) * (eye + r)
        pair = split(r)
        r = rows[0][0] * dot3(pair, pair) - rows[0][1] * eye
        for n, (a, c) in enumerate(rows[1:], 1):
            pair, halves = split(r), split(x)
            if n < FULL:
                moved, square = dot3(halves, pair), dot3(pair, pair)
            else:
                moved = dot(halves[0], pair[0]) + dot(halves[1], pair[0])
                square = dot(pair[0], pair[0])
            if jobs:
                jobs.pop(0)()
            x = a * (x + moved)
            r = a * square - c * eye
        left = eye - dot6(tiles[k, k], x)
        for job in jobs:
            job()
        halves, left = split(x), left.astype(BF16)
        return x + (dot(halves[0], left) + dot(halves[1], left))

    def product(a, b, dims, k):
        return dot6(a, b, dims) if k == 0 else dot3(split(a), split(b), dims)

    def lower(i, k, inv):
        low[i, k] = product(tiles[i, k], inv, NN, k)

    def update(i, j, k):
        tiles[i, j] = tiles[i, j] - product(low[i, k], tiles[j, k], NT, k)

    def put(k, value):
        high, rest = split(value)
        g_mat[0, :, k * size : (k + 1) * size] = high
        g_mat[1, :, k * size : (k + 1) * size] = rest

    inv = inverse(0)
    covariance(3, 0)
    lower(3, 0, inv)

    @pl.when(g == 0)
    def _():
        own_obs.wait()

    @pl.when(g != 0)
    def _():
        column_obs[0].wait_recv()

    mine_loc.wait()
    every_loc.wait_recv()
    mine_obs = local_copy(col_obs, all_obs.at[d], 3)
    every_obs = spread(col_obs, all_obs, 10, 5)
    pts[1] = points(all_loc[jnp.maximum(wi, 0)])
    pts[2] = points(all_loc[jnp.maximum(wj, 0)])
    covariance(1, 0)
    covariance(1, 1)
    lower(1, 0, inv)
    update(1, 1, 0)

    def one():
        covariance(2, 0)
        lower(2, 0, inv)

    def two():
        covariance(2, 1)
        update(2, 1, 0)

    def three():
        covariance(2, 2)
        update(2, 2, 0)

    def fifth():
        update(3, 3, 0)

    def four():
        covariance(3, 1)
        update(3, 1, 0)

    def five():
        covariance(3, 2)
        update(3, 2, 0)

    inv1 = inverse(1, (one, two, three, four, five, fifth))
    lower(2, 1, inv1)
    update(2, 2, 1)

    def six():
        lower(3, 1, inv1)

    def seven():
        update(3, 2, 1)

    def eight():
        update(3, 3, 1)

    def nine():
        low[2, 0] = dot6(low[2, 1], low[1, 0]) - low[2, 0]

    def ten():
        low[3, 0] = dot6(low[3, 1], low[1, 0]) - low[3, 0]

    inv2 = inverse(2, (six, seven, eight, nine, ten))
    lower(3, 2, inv2)
    update(3, 3, 2)

    def eleven():
        put(2, -low[3, 2])

    def twelve():
        put(1, dot6(low[3, 2], low[2, 1]) - low[3, 1])

    def thirteen():
        put(0, low[3, 0] - dot6(low[3, 2], low[2, 0]))

    def dot_small(rows, mat, dims):
        high, rest = split(rows)
        return dot(high, mat[0], dims) + (dot(high, mat[1], dims) + dot(rest, mat[0], dims))

    def forward(own, before_rows, table):
        slots = jnp.concatenate(
            [before_rows, table[jnp.maximum(wi, 0)], table[jnp.maximum(wj, 0)]], axis=1
        )
        return own + dot_small(slots, g_mat, NT)

    def fourteen():
        pre[...] = forward(obs_v[...], prev_obs[...], all_obs)

    ahead_obs.wait()
    mine_obs.wait()
    every_obs.wait_recv()
    inv3 = inverse(3, (eleven, twelve, thirteen, fourteen))
    p_mat[0], p_mat[1] = split(inv3)

    def reduce(u, own, row, k, filler):
        hop[k] = u[:, :size]
        half = size // 2
        ui, uj = u[:, size : 2 * size], u[:, 2 * size :]

        def fill(m):
            fi = jnp.where(wi == m, 1.0, 0.0).astype(F32)
            fj = jnp.where(wj == m, 1.0, 0.0).astype(F32)
            block = fi * ui + fj * uj
            msg[k, m, :fields] = block[:, :half]
            msg[k, m, fields : 2 * fields] = block[:, half:]
            msg[k, m, 2 * fields :] = row

        returned = remote(hop.at[k], back.at[k], sem_s.at[11], sem_r.at[6 + k], before)
        targets = plane + [d]
        for m in targets[:LEAD]:
            fill(m)
        returned.start()
        for n, m in enumerate(plane):
            if n + LEAD < DEV:
                fill(targets[n + LEAD])
            remote(
                msg.at[k, m], rs.at[k, d], sem_s.at[12], sem_r.at[8 + k], {"grp": g, "dev": m}
            ).start()
        mine = local_copy(msg.at[k, d], rs.at[k, d], 0)
        filler()
        piece = rs.at[k, others]
        every = remote(piece, piece, sem_s.at[12], sem_r.at[8 + k], after)
        returned.wait()
        own = own + back[k]
        every.wait_recv()
        mine.wait()
        sums = [rs[k, n] for n in range(4)]
        for n in range(4, DEV):
            sums[n % 4] = sums[n % 4] + rs[k, n]
        total = (sums[0] + sums[1]) + (sums[2] + sums[3])
        held = first_group * jnp.concatenate(
            [own[:, :half], own[:, half:], jnp.zeros((1, half), F32)], axis=0
        )
        total = total + held
        xs[k, g] = total
        stage[k] = total
        copies = [
            remote(
                stage.at[k], xs.at[k, g], sem_s.at[12 + n], sem_r.at[9 + n + 3 * k],
                {"grp": lax.rem(g + n, GRP), "dev": d},
            )
            for n in (2, 1, 3)
        ]
        for c in copies:
            c.start()
        every.wait_send()
        for c in copies:
            c.wait()
        total = (xs[k, 0] + xs[k, 1]) + (xs[k, 2] + xs[k, 3])
        column = jnp.concatenate([total[:fields], total[fields : 2 * fields]], axis=1)
        image = jnp.where(g == 0, column, own)
        return image, column, total[2 * fields :]

    b, prec = obs_v[...], noise_v[...]
    v0 = pre[...]
    w0 = dot_small(v0, p_mat, NN)
    u0 = dot_small(w0, g_mat, NN)
    kept = prec * b

    def joined():
        left = (p_mat[0], p_mat[1])
        for k in range(3):
            cut = slice(k * size, (k + 1) * size)
            h_mat[0, :, cut], h_mat[1, :, cut] = split(
                dot3(left, (g_mat[0, :, cut], g_mat[1, :, cut]))
            )

    image0, column, row = reduce(u0, w0 + kept, to_row([b * b, v0 * w0 + kept * b]), 0, joined)
    rr0, p0 = from_row(row, 0, fields), from_row(row, 1, fields)
    alpha0 = rr0 / p0
    r1 = b - alpha0 * image0
    rcol[0] = r1
    rcol[1] = col_obs[...] - alpha0 * column
    ahead = remote(rcol.at[0], prev1, sem_s.at[11], sem_r.at[16], after)
    ahead.start()
    mine = local_copy(rcol.at[1], ag.at[d], 0)
    every = spread(rcol.at[1], ag, 12, 17)
    ahead.wait()
    mine.wait()
    every.wait()
    v1 = forward(r1, prev1[...], ag)
    w1 = dot_small(v1, p_mat, NN)
    u1 = dot_small(v1, h_mat, NN)
    kept = prec * r1
    image1, column, row = reduce(
        u1, w1 + kept, to_row([v1 * w1 + kept * r1, v1 * w0 + kept * b, r1 * r1]), 1,
        lambda: None,
    )
    s1, s2, rr1 = (from_row(row, k, fields) for k in range(3))
    beta = rr1 / rr0
    alpha1 = rr1 / (s1 + 2.0 * beta * s2 + beta * beta * p0)
    image1 = image1 + beta * image0
    out[0] = alpha0 * b + alpha1 * (r1 + beta * b)
    out[1] = r1 - alpha1 * image1
    every_loc.wait_send()
    every_obs.wait_send()

    @pl.when(g == 0)
    def _():
        for c in column_loc + column_obs:
            c.wait_send()


def local(locations, neighbours, observations, noise_prec):
    points, fields = locations.shape[2], observations.shape[1]
    vmem = pl.BlockSpec(memory_space=pltpu.VMEM)
    hbm = pl.BlockSpec(memory_space=pltpu.HBM)

    def f32(*shape):
        return pltpu.VMEM(shape, F32)

    tall = 2 * fields + 1
    held = [
        pltpu.with_memory_space_constraint(x, pltpu.HBM)
        for x in (neighbours, jnp.transpose(locations, (1, 0, 2)), observations, noise_prec)
    ]
    both = pl.pallas_call(
        kernel,
        out_shape=jax.ShapeDtypeStruct((2, fields, points), F32),
        in_specs=[hbm] * 4,
        out_specs=vmem,
        scratch_shapes=[
            pltpu.SMEM((1, neighbours.shape[1]), jnp.int32),
            f32(3, 1, points), f32(fields, points), f32(fields, points),
            f32(3, 1, points), f32(fields, points),
            f32(3, 1, points), f32(fields, points),
            f32(DEV, 3, 1, points), f32(DEV, fields, points),
            f32(4, 4, points, points), f32(4, 3, points, points),
            pltpu.VMEM((2, points, 3 * points), BF16), pltpu.VMEM((2, points, points), BF16),
            pltpu.VMEM((2, points, 3 * points), BF16), f32(fields, points),
            f32(2, DEV, tall, points // 2), f32(2, DEV, tall, points // 2),
            f32(2, GRP, tall, points // 2), f32(2, tall, points // 2),
            f32(2, fields, points), f32(2, fields, points),
            f32(2, fields, points), f32(fields, points), f32(DEV, fields, points),
            pltpu.SemaphoreType.DMA((4,)),
            pltpu.SemaphoreType.DMA((4,)),
            pltpu.SemaphoreType.DMA((16,)),
            pltpu.SemaphoreType.DMA((18,)),
        ],
        compiler_params=pltpu.CompilerParams(
            collective_id=0, has_side_effects=True, vmem_limit_bytes=48 << 20
        ),
    )(*held)
    return both[:1], both[1:]


def solution(mesh):
    placed = (
        P(("grp", "dev"), None, None),
        P(("grp", "dev"), None),
        P(("grp", "dev"), None, None),
        P(("grp", "dev"), None, None),
    )
    return jax.shard_map(
        local,
        mesh=mesh,
        in_specs=placed,
        out_specs=(P(("grp", "dev"), None, None), P(("grp", "dev"), None, None)),
        check_vma=False,
    )
```

```python
import math

import jax
import jax.numpy as jnp
from jax import lax
from jax.experimental import pallas as pl
from jax.experimental.pallas import tpu as pltpu
from jax.sharding import PartitionSpec as P

SCALE_LENGTH = 0.5
NUGGET = 0.5
SQRT_THREE = math.sqrt(3.0)
F32 = jnp.float32
BF16 = jnp.bfloat16
NN = (((1,), (0,)), ((), ()))
NT = (((1,), (1,)), ((), ()))
DOUBLINGS, FULL, LEAD = 7, 4, 6
GRP, DEV = 4, 32


def coefficients(size):
    low, high = NUGGET, size + NUGGET
    tau = (high + low) / (high - low)
    rows = []
    for _ in range(DOUBLINGS):
        twice = 2.0 * tau * tau - 1.0
        rows.append((2.0 * tau * tau / twice, 1.0 / twice))
        tau = twice
    return rows, 2.0 / (high + low)


def pick(values, n):
    out = jnp.float32(values[-1])
    for k in range(len(values) - 2, -1, -1):
        out = jnp.where(n == k, jnp.float32(values[k]), out)
    return out


def split(x):
    high = x.astype(BF16)
    return high, (x - high.astype(F32)).astype(BF16)


def dot(a, b, dims=NN):
    return lax.dot_general(a, b, dims, preferred_element_type=F32)


def dot3(a, b, dims=NN):
    return dot(a[0], b[0], dims) + (dot(a[0], b[1], dims) + dot(a[1], b[0], dims))


def dot6(a, b, dims=NN):
    return lax.dot_general(
        a, b, dims, preferred_element_type=F32, precision=lax.Precision.HIGHEST
    )


def neighbourhood():
    g, d = lax.axis_index("grp"), lax.axis_index("dev")
    flat = g * DEV + d
    after, before = lax.rem(flat + 1, GRP * DEV), lax.rem(flat + GRP * DEV - 1, GRP * DEV)
    return g, d, place(after), place(before)


def mates(d):
    far = (2, 1, 3, 0)
    y, z, c = d // 8, lax.rem(d // 2, 4), lax.rem(d, 2)
    ys = {k: lax.rem(y + k, 4) * 8 for k in far}
    zs = {k: lax.rem(z + k, 4) * 2 for k in far}
    cs = {1: 1 - c, 0: c}
    return [ys[a] + (zs[b] + cs[e]) for a in far for b in far for e in (1, 0)][:-1]


def place(flat):
    return {"grp": flat // DEV, "dev": lax.rem(flat, DEV)}


def greet(g, d, plane, after, before):
    barrier = pltpu.get_barrier_semaphore()
    for k in (2, 1, 3):
        pl.semaphore_signal(barrier, 1, device_id={"grp": lax.rem(g + k, GRP), "dev": d})
    pl.semaphore_signal(barrier, 1, device_id=before)
    pl.semaphore_signal(barrier, 1, device_id=after)
    for m in plane:
        pl.semaphore_signal(barrier, 1, device_id={"grp": g, "dev": m})
    return barrier


def remote(src, dst, send, recv, device):
    return pltpu.make_async_remote_copy(
        src_ref=src, dst_ref=dst, send_sem=send, recv_sem=recv, device_id=device
    )


def lane(shape):
    return lax.broadcasted_iota(jnp.int32, shape, 1)


def sublane(shape):
    return lax.broadcasted_iota(jnp.int32, shape, 0)


def to_row(parts):
    fields = parts[0].shape[0]
    spread = jnp.zeros((fields, 128), F32)
    slot = lane(spread.shape) - sublane(spread.shape)
    for k, part in enumerate(parts):
        spread = jnp.where(slot == k * fields, jnp.sum(part, axis=1, keepdims=True), spread)
    return jnp.sum(spread, axis=0, keepdims=True)


def from_row(row, k, fields):
    spread = jnp.broadcast_to(row, (fields, 128))
    slot = lane(spread.shape) - sublane(spread.shape)
    return jnp.sum(jnp.where(slot == k * fields, spread, 0.0), axis=1, keepdims=True)


def kernel(
    near_hbm, loc, obs, noise,
    out,
    near, loc_v, obs_v, noise_v, prev_loc, prev_obs, col_loc, col_obs, all_loc, all_obs,
    tiles, low, g_mat, p_mat, h_mat, pre,
    msg, rs, xs, stage, hop, back, rcol, prev1, ag,
    sem_in, sem_mine, sem_s, sem_r,
):
    fields, size = obs_v.shape
    g, d, after, before = neighbourhood()
    plane = mates(d)
    barrier = greet(g, d, plane, after, before)
    incoming = [
        pltpu.make_async_copy(src, dst, sem_in.at[k])
        for k, (src, dst) in enumerate(
            ((loc, loc_v), (near_hbm, near), (obs.at[0], obs_v), (noise.at[0], noise_v))
        )
    ]
    for c in incoming:
        c.start()
    others = pl.ds(0, DEV - 1)
    eye = (sublane((size, size)) == lane((size, size))).astype(F32)
    rows, first = coefficients(size)
    first_group = jnp.where(g == 0, 1.0, 0.0).astype(F32)
    def points(value):
        flat = [value[c] for c in range(3)]
        upright = jnp.concatenate(flat + [jnp.zeros((5, size), F32)], axis=0).T
        return flat, upright

    def covariance(i, j):
        total = None
        for c in range(3):
            offset = pts[i][1][:, c : c + 1] - pts[j][0][c]
            total = offset * offset if total is None else total + offset * offset
        scaled = (SQRT_THREE / SCALE_LENGTH) * jnp.sqrt(total)
        value = (1.0 + scaled) * jnp.exp(-scaled) * (live[i] * live[j])
        if i == j:
            value = value + eye * (NUGGET * live[i] + (1.0 - live[i]))
        tiles[i, j] = value

    def spread(src, dst, s, r):
        for m in plane:
            remote(src, dst.at[d], sem_s.at[s], sem_r.at[r], {"grp": g, "dev": m}).start()
        piece = dst.at[others]
        return remote(piece, piece, sem_s.at[s], sem_r.at[r], after)

    def local_copy(src, dst, k):
        c = pltpu.make_async_copy(src, dst, sem_mine.at[k])
        c.start()
        return c

    pl.semaphore_wait(barrier, DEV - 1 + GRP - 1 + 2)
    ahead_loc = remote(loc, prev_loc, sem_s.at[0], sem_r.at[0], after)
    column_loc = [
        remote(loc, col_loc, sem_s.at[1 + k], sem_r.at[1], {"grp": k, "dev": d})
        for k in range(1, GRP)
    ]
    own_loc = pltpu.make_async_copy(loc, col_loc, sem_mine.at[0])
    ahead_obs = remote(obs.at[0], prev_obs, sem_s.at[5], sem_r.at[2], after)
    column_obs = [
        remote(obs.at[0], col_obs, sem_s.at[5 + k], sem_r.at[3], {"grp": k, "dev": d})
        for k in range(1, GRP)
    ]
    own_obs = pltpu.make_async_copy(obs.at[0], col_obs, sem_mine.at[1])

    @pl.when(g == 0)
    def _():
        column_loc[1].start()
        column_loc[0].start()
        column_loc[2].start()
        own_loc.start()

    ahead_loc.start()
    incoming[0].wait()
    incoming[1].wait()
    wi, wj = near[0, 2], near[0, 3]
    live = [jnp.where(near[0, s] >= 0, 1.0, 0.0).astype(F32) for s in (0, 2, 3)] + [1.0]
    pts = [None, None, None, points(loc_v)]
    covariance(3, 3)
    incoming[2].wait()
    incoming[3].wait()

    @pl.when(g == 0)
    def _():
        own_loc.wait()

    @pl.when(g != 0)
    def _():
        column_loc[0].wait_recv()

    mine_loc = local_copy(col_loc, all_loc.at[d], 2)
    every_loc = spread(col_loc, all_loc, 9, 4)
    ahead_obs.start()

    @pl.when(g == 0)
    def _():
        for c in column_obs:
            c.start()
        own_obs.start()

    ahead_loc.wait()
    pts[0] = points(prev_loc)
    covariance(0, 0)
    def inverse(k, jobs=()):
        jobs = list(jobs)
        e = first * tiles[k, k]
        x = (first * rows[0][0]) * (2.0 * eye - e)
        pair = split(e)
        e = rows[0][0] * (2.0 * e - dot3(pair, pair))
        for n, (a, c) in enumerate(rows[1:], 1):
            halves = split(x)
            if n < FULL:
                pair = split(e)
                moved, square = dot3(halves, pair), dot3(pair, pair)
            else:
                r = (eye - e if n == FULL else r).astype(BF16)
                moved, square = dot(halves[0], r) + dot(halves[1], r), dot(r, r)
            if jobs:
                jobs.pop(0)()
            if n < FULL:
                x, e = a * (2.0 * x - moved), a * (2.0 * e - square)
            else:
                x, r = a * (x + moved), a * square - c * eye
        left = eye - dot6(tiles[k, k], x) if k == 3 else None
        for job in jobs:
            job()
        if k < 3:
            return x
        halves, left = split(x), left.astype(BF16)
        return x + (dot(halves[0], left) + dot(halves[1], left))

    def lower(i, k, inv):
        panel, pair = tiles[i, k], split(inv)
        value = dot3(split(panel), pair)
        left = panel - dot6(value, tiles[k, k])
        low[i, k] = value + dot3(split(left), pair)

    def update(i, j, k):
        tiles[i, j] = tiles[i, j] - dot3(split(low[i, k]), split(tiles[j, k]), NT)

    def put(k, value):
        high, rest = split(value)
        g_mat[0, :, k * size : (k + 1) * size] = high
        g_mat[1, :, k * size : (k + 1) * size] = rest

    inv = inverse(0)
    covariance(3, 0)
    lower(3, 0, inv)

    @pl.when(g == 0)
    def _():
        own_obs.wait()

    @pl.when(g != 0)
    def _():
        column_obs[0].wait_recv()

    mine_loc.wait()
    every_loc.wait_recv()
    mine_obs = local_copy(col_obs, all_obs.at[d], 3)
    every_obs = spread(col_obs, all_obs, 10, 5)
    pts[1] = points(all_loc[jnp.maximum(wi, 0)])
    pts[2] = points(all_loc[jnp.maximum(wj, 0)])
    covariance(1, 0)
    covariance(1, 1)
    lower(1, 0, inv)
    update(1, 1, 0)

    def one():
        covariance(2, 0)
        lower(2, 0, inv)

    def two():
        covariance(2, 1)
        update(2, 1, 0)

    def three():
        covariance(2, 2)
        update(2, 2, 0)

    def fifth():
        update(3, 3, 0)

    def four():
        covariance(3, 1)
        update(3, 1, 0)

    def five():
        covariance(3, 2)
        update(3, 2, 0)

    inv1 = inverse(1, (one, two, three, four, five, fifth))
    lower(2, 1, inv1)
    update(2, 2, 1)

    def six():
        lower(3, 1, inv1)

    def seven():
        update(3, 2, 1)

    def eight():
        update(3, 3, 1)

    def nine():
        low[2, 0] = dot3(split(low[2, 1]), split(low[1, 0])) - low[2, 0]

    def ten():
        low[3, 0] = dot3(split(low[3, 1]), split(low[1, 0])) - low[3, 0]

    inv2 = inverse(2, (six, seven, eight, nine, ten))
    lower(3, 2, inv2)
    update(3, 3, 2)

    def eleven():
        put(2, -low[3, 2])

    def twelve():
        put(1, dot3(split(low[3, 2]), split(low[2, 1])) - low[3, 1])

    def thirteen():
        put(0, low[3, 0] - dot3(split(low[3, 2]), split(low[2, 0])))

    def dot_small(rows, mat, dims):
        high, rest = split(rows)
        return dot(high, mat[0], dims) + (dot(high, mat[1], dims) + dot(rest, mat[0], dims))

    def forward(own, before_rows, table):
        slots = jnp.concatenate(
            [before_rows, table[jnp.maximum(wi, 0)], table[jnp.maximum(wj, 0)]], axis=1
        )
        return own + dot_small(slots, g_mat, NT)

    def fourteen():
        pre[...] = forward(obs_v[...], prev_obs[...], all_obs)

    ahead_obs.wait()
    mine_obs.wait()
    every_obs.wait_recv()
    inv3 = inverse(3, (eleven, twelve, thirteen, fourteen))
    p_mat[0], p_mat[1] = split(inv3)

    def reduce(u, own, row, k, filler):
        hop[k] = u[:, :size]
        half = size // 2
        ui, uj = u[:, size : 2 * size], u[:, 2 * size :]

        def fill(m):
            fi = jnp.where(wi == m, 1.0, 0.0).astype(F32)
            fj = jnp.where(wj == m, 1.0, 0.0).astype(F32)
            block = fi * ui + fj * uj
            msg[k, m, :fields] = block[:, :half]
            msg[k, m, fields : 2 * fields] = block[:, half:]
            msg[k, m, 2 * fields :] = row

        returned = remote(hop.at[k], back.at[k], sem_s.at[11], sem_r.at[6 + k], before)
        targets = plane + [d]
        for m in targets[:LEAD]:
            fill(m)
        returned.start()
        for n, m in enumerate(plane):
            if n + LEAD < DEV:
                fill(targets[n + LEAD])
            remote(
                msg.at[k, m], rs.at[k, d], sem_s.at[12], sem_r.at[8 + k], {"grp": g, "dev": m}
            ).start()
        mine = local_copy(msg.at[k, d], rs.at[k, d], 0)
        filler()
        piece = rs.at[k, others]
        every = remote(piece, piece, sem_s.at[12], sem_r.at[8 + k], after)
        returned.wait()
        own = own + back[k]
        every.wait_recv()
        mine.wait()
        sums = [rs[k, n] for n in range(4)]
        for n in range(4, DEV):
            sums[n % 4] = sums[n % 4] + rs[k, n]
        total = (sums[0] + sums[1]) + (sums[2] + sums[3])
        held = first_group * jnp.concatenate(
            [own[:, :half], own[:, half:], jnp.zeros((1, half), F32)], axis=0
        )
        total = total + held
        xs[k, g] = total
        stage[k] = total
        copies = [
            remote(
                stage.at[k], xs.at[k, g], sem_s.at[12 + n], sem_r.at[9 + n + 3 * k],
                {"grp": lax.rem(g + n, GRP), "dev": d},
            )
            for n in (2, 1, 3)
        ]
        for c in copies:
            c.start()
        every.wait_send()
        for c in copies:
            c.wait()
        total = (xs[k, 0] + xs[k, 1]) + (xs[k, 2] + xs[k, 3])
        column = jnp.concatenate([total[:fields], total[fields : 2 * fields]], axis=1)
        image = jnp.where(g == 0, column, own)
        return image, column, total[2 * fields :]

    b, prec = obs_v[...], noise_v[...]
    v0 = pre[...]
    w0 = dot_small(v0, p_mat, NN)
    u0 = dot_small(w0, g_mat, NN)
    kept = prec * b

    def joined():
        left = (p_mat[0], p_mat[1])
        for k in range(3):
            cut = slice(k * size, (k + 1) * size)
            h_mat[0, :, cut], h_mat[1, :, cut] = split(
                dot3(left, (g_mat[0, :, cut], g_mat[1, :, cut]))
            )

    image0, column, row = reduce(u0, w0 + kept, to_row([b * b, v0 * w0 + kept * b]), 0, joined)
    rr0, p0 = from_row(row, 0, fields), from_row(row, 1, fields)
    alpha0 = rr0 / p0
    r1 = b - alpha0 * image0
    rcol[0] = r1
    rcol[1] = col_obs[...] - alpha0 * column
    ahead = remote(rcol.at[0], prev1, sem_s.at[11], sem_r.at[16], after)
    ahead.start()
    mine = local_copy(rcol.at[1], ag.at[d], 0)
    every = spread(rcol.at[1], ag, 12, 17)
    ahead.wait()
    mine.wait()
    every.wait()
    v1 = forward(r1, prev1[...], ag)
    w1 = dot_small(v1, p_mat, NN)
    u1 = dot_small(v1, h_mat, NN)
    kept = prec * r1
    image1, column, row = reduce(
        u1, w1 + kept, to_row([v1 * w1 + kept * r1, v1 * w0 + kept * b, r1 * r1]), 1,
        lambda: None,
    )
    s1, s2, rr1 = (from_row(row, k, fields) for k in range(3))
    beta = rr1 / rr0
    alpha1 = rr1 / (s1 + 2.0 * beta * s2 + beta * beta * p0)
    image1 = image1 + beta * image0
    out[0] = alpha0 * b + alpha1 * (r1 + beta * b)
    out[1] = r1 - alpha1 * image1
    every_loc.wait_send()
    every_obs.wait_send()

    @pl.when(g == 0)
    def _():
        for c in column_loc + column_obs:
            c.wait_send()


def local(locations, neighbours, observations, noise_prec):
    points, fields = locations.shape[2], observations.shape[1]
    vmem = pl.BlockSpec(memory_space=pltpu.VMEM)
    hbm = pl.BlockSpec(memory_space=pltpu.HBM)

    def f32(*shape):
        return pltpu.VMEM(shape, F32)

    tall = 2 * fields + 1
    held = [
        pltpu.with_memory_space_constraint(x, pltpu.HBM)
        for x in (neighbours, jnp.transpose(locations, (1, 0, 2)), observations, noise_prec)
    ]
    both = pl.pallas_call(
        kernel,
        out_shape=jax.ShapeDtypeStruct((2, fields, points), F32),
        in_specs=[hbm] * 4,
        out_specs=vmem,
        scratch_shapes=[
            pltpu.SMEM((1, neighbours.shape[1]), jnp.int32),
            f32(3, 1, points), f32(fields, points), f32(fields, points),
            f32(3, 1, points), f32(fields, points),
            f32(3, 1, points), f32(fields, points),
            f32(DEV, 3, 1, points), f32(DEV, fields, points),
            f32(4, 4, points, points), f32(4, 3, points, points),
            pltpu.VMEM((2, points, 3 * points), BF16), pltpu.VMEM((2, points, points), BF16),
            pltpu.VMEM((2, points, 3 * points), BF16), f32(fields, points),
            f32(2, DEV, tall, points // 2), f32(2, DEV, tall, points // 2),
            f32(2, GRP, tall, points // 2), f32(2, tall, points // 2),
            f32(2, fields, points), f32(2, fields, points),
            f32(2, fields, points), f32(fields, points), f32(DEV, fields, points),
            pltpu.SemaphoreType.DMA((4,)),
            pltpu.SemaphoreType.DMA((4,)),
            pltpu.SemaphoreType.DMA((16,)),
            pltpu.SemaphoreType.DMA((18,)),
        ],
        compiler_params=pltpu.CompilerParams(
            collective_id=0, has_side_effects=True, vmem_limit_bytes=48 << 20
        ),
    )(*held)
    return both[:1], both[1:]


def solution(mesh):
    placed = (
        P(("grp", "dev"), None, None),
        P(("grp", "dev"), None),
        P(("grp", "dev"), None, None),
        P(("grp", "dev"), None, None),
    )
    return jax.shard_map(
        local,
        mesh=mesh,
        in_specs=placed,
        out_specs=(P(("grp", "dev"), None, None), P(("grp", "dev"), None, None)),
        check_vma=False,
    )
```

```python
import math

import jax
import jax.numpy as jnp
from jax import lax
from jax.experimental import pallas as pl
from jax.experimental.pallas import tpu as pltpu
from jax.sharding import PartitionSpec as P

SCALE_LENGTH = 0.5
NUGGET = 0.5
SQRT_THREE = math.sqrt(3.0)
F32 = jnp.float32
BF16 = jnp.bfloat16
NN = (((1,), (0,)), ((), ()))
NT = (((1,), (1,)), ((), ()))
DOUBLINGS, FULL, LEAD = 7, 4, 6
GRP, DEV = 4, 32


def coefficients(size):
    low, high = NUGGET, size + NUGGET
    tau = (high + low) / (high - low)
    rows = []
    for _ in range(DOUBLINGS):
        twice = 2.0 * tau * tau - 1.0
        rows.append((2.0 * tau * tau / twice, 1.0 / twice))
        tau = twice
    return rows, 2.0 / (high + low)


def pick(values, n):
    out = jnp.float32(values[-1])
    for k in range(len(values) - 2, -1, -1):
        out = jnp.where(n == k, jnp.float32(values[k]), out)
    return out


def split(x):
    high = x.astype(BF16)
    return high, (x - high.astype(F32)).astype(BF16)


def dot(a, b, dims=NN):
    return lax.dot_general(a, b, dims, preferred_element_type=F32)


def dot3(a, b, dims=NN):
    return dot(a[0], b[0], dims) + (dot(a[0], b[1], dims) + dot(a[1], b[0], dims))


def dot6(a, b, dims=NN):
    return lax.dot_general(
        a, b, dims, preferred_element_type=F32, precision=lax.Precision.HIGHEST
    )


def neighbourhood():
    g, d = lax.axis_index("grp"), lax.axis_index("dev")
    flat = g * DEV + d
    after, before = lax.rem(flat + 1, GRP * DEV), lax.rem(flat + GRP * DEV - 1, GRP * DEV)
    return g, d, place(after), place(before)


def mates(d):
    far = (2, 1, 3, 0)
    y, z, c = d // 8, lax.rem(d // 2, 4), lax.rem(d, 2)
    ys = {k: lax.rem(y + k, 4) * 8 for k in far}
    zs = {k: lax.rem(z + k, 4) * 2 for k in far}
    cs = {1: 1 - c, 0: c}
    return [ys[a] + (zs[b] + cs[e]) for a in far for b in far for e in (1, 0)][:-1]


def place(flat):
    return {"grp": flat // DEV, "dev": lax.rem(flat, DEV)}


def greet(g, d, plane, after, before):
    barrier = pltpu.get_barrier_semaphore()
    for k in (2, 1, 3):
        pl.semaphore_signal(barrier, 1, device_id={"grp": lax.rem(g + k, GRP), "dev": d})
    pl.semaphore_signal(barrier, 1, device_id=before)
    pl.semaphore_signal(barrier, 1, device_id=after)
    for m in plane:
        pl.semaphore_signal(barrier, 1, device_id={"grp": g, "dev": m})
    return barrier


def remote(src, dst, send, recv, device):
    return pltpu.make_async_remote_copy(
        src_ref=src, dst_ref=dst, send_sem=send, recv_sem=recv, device_id=device
    )


def lane(shape):
    return lax.broadcasted_iota(jnp.int32, shape, 1)


def sublane(shape):
    return lax.broadcasted_iota(jnp.int32, shape, 0)


def to_row(parts):
    fields = parts[0].shape[0]
    spread = jnp.zeros((fields, 128), F32)
    slot = lane(spread.shape) - sublane(spread.shape)
    for k, part in enumerate(parts):
        spread = jnp.where(slot == k * fields, jnp.sum(part, axis=1, keepdims=True), spread)
    return jnp.sum(spread, axis=0, keepdims=True)


def from_row(row, k, fields):
    spread = jnp.broadcast_to(row, (fields, 128))
    slot = lane(spread.shape) - sublane(spread.shape)
    return jnp.sum(jnp.where(slot == k * fields, spread, 0.0), axis=1, keepdims=True)


def kernel(
    near_hbm, loc, obs, noise,
    out,
    near, loc_v, obs_v, noise_v, prev_loc, prev_obs, col_loc, col_obs, all_loc, all_obs,
    tiles, low, g_mat, p_mat, h_mat, pre,
    msg, rs, xs, stage, hop, back, rcol, prev1, ag,
    sem_in, sem_mine, sem_s, sem_r,
):
    fields, size = obs_v.shape
    g, d, after, before = neighbourhood()
    plane = mates(d)
    barrier = greet(g, d, plane, after, before)
    incoming = [
        pltpu.make_async_copy(src, dst, sem_in.at[k])
        for k, (src, dst) in enumerate(
            ((loc, loc_v), (near_hbm, near), (obs.at[0], obs_v), (noise.at[0], noise_v))
        )
    ]
    for c in incoming:
        c.start()
    others = pl.ds(0, DEV - 1)
    eye = (sublane((size, size)) == lane((size, size))).astype(F32)
    rows, first = coefficients(size)
    first_group = jnp.where(g == 0, 1.0, 0.0).astype(F32)
    def points(value):
        flat = [value[c] for c in range(3)]
        upright = jnp.concatenate(flat + [jnp.zeros((5, size), F32)], axis=0).T
        return flat, upright

    def covariance(i, j):
        total = None
        for c in range(3):
            offset = pts[i][1][:, c : c + 1] - pts[j][0][c]
            total = offset * offset if total is None else total + offset * offset
        scaled = (SQRT_THREE / SCALE_LENGTH) * jnp.sqrt(total)
        value = (1.0 + scaled) * jnp.exp(-scaled) * (live[i] * live[j])
        if i == j:
            value = value + eye * (NUGGET * live[i] + (1.0 - live[i]))
        tiles[i, j] = value

    def spread(src, dst, s, r):
        for m in plane:
            remote(src, dst.at[d], sem_s.at[s], sem_r.at[r], {"grp": g, "dev": m}).start()
        piece = dst.at[others]
        return remote(piece, piece, sem_s.at[s], sem_r.at[r], after)

    def local_copy(src, dst, k):
        c = pltpu.make_async_copy(src, dst, sem_mine.at[k])
        c.start()
        return c

    pl.semaphore_wait(barrier, DEV - 1 + GRP - 1 + 2)
    ahead_loc = remote(loc, prev_loc, sem_s.at[0], sem_r.at[0], after)
    column_loc = [
        remote(loc, col_loc, sem_s.at[1 + k], sem_r.at[1], {"grp": k, "dev": d})
        for k in range(1, GRP)
    ]
    own_loc = pltpu.make_async_copy(loc, col_loc, sem_mine.at[0])
    ahead_obs = remote(obs.at[0], prev_obs, sem_s.at[5], sem_r.at[2], after)
    column_obs = [
        remote(obs.at[0], col_obs, sem_s.at[5 + k], sem_r.at[3], {"grp": k, "dev": d})
        for k in range(1, GRP)
    ]
    own_obs = pltpu.make_async_copy(obs.at[0], col_obs, sem_mine.at[1])

    @pl.when(g == 0)
    def _():
        column_loc[1].start()
        column_loc[0].start()
        column_loc[2].start()
        own_loc.start()

    ahead_loc.start()
    incoming[0].wait()
    incoming[1].wait()
    wi, wj = near[0, 2], near[0, 3]
    live = [jnp.where(near[0, s] >= 0, 1.0, 0.0).astype(F32) for s in (0, 2, 3)] + [1.0]
    pts = [None, None, None, points(loc_v)]
    covariance(3, 3)
    incoming[2].wait()
    incoming[3].wait()

    @pl.when(g == 0)
    def _():
        own_loc.wait()

    @pl.when(g != 0)
    def _():
        column_loc[0].wait_recv()

    mine_loc = local_copy(col_loc, all_loc.at[d], 2)
    every_loc = spread(col_loc, all_loc, 9, 4)
    ahead_obs.start()

    @pl.when(g == 0)
    def _():
        for c in column_obs:
            c.start()
        own_obs.start()

    ahead_loc.wait()
    pts[0] = points(prev_loc)
    covariance(0, 0)
    def inverse(k, jobs=()):
        jobs = list(jobs)
        e = first * tiles[k, k]
        x = (first * rows[0][0]) * (2.0 * eye - e)
        pair = split(e)
        e = rows[0][0] * (2.0 * e - dot3(pair, pair))
        for n, (a, c) in enumerate(rows[1:], 1):
            halves = split(x)
            if n < FULL:
                pair = split(e)
                moved, square = dot3(halves, pair), dot3(pair, pair)
            else:
                r = (eye - e if n == FULL else r).astype(BF16)
                moved, square = dot(halves[0], r) + dot(halves[1], r), dot(r, r)
            if jobs:
                jobs.pop(0)()
            if n < FULL:
                x, e = a * (2.0 * x - moved), a * (2.0 * e - square)
            else:
                x, r = a * (x + moved), a * square - c * eye
        left = eye - dot6(tiles[k, k], x) if k == 3 else None
        for job in jobs:
            job()
        if k < 3:
            return x
        halves, left = split(x), left.astype(BF16)
        return x + (dot(halves[0], left) + dot(halves[1], left))

    def lower(i, k, inv):
        panel, pair = tiles[i, k], split(inv)
        value = dot3(split(panel), pair)
        left = panel - dot6(value, tiles[k, k])
        low[i, k] = value + dot3(split(left), pair)

    def update(i, j, k):
        tiles[i, j] = tiles[i, j] - dot3(split(low[i, k]), split(tiles[j, k]), NT)

    def put(k, value):
        high, rest = split(value)
        g_mat[0, :, k * size : (k + 1) * size] = high
        g_mat[1, :, k * size : (k + 1) * size] = rest

    inv = inverse(0)
    covariance(3, 0)
    lower(3, 0, inv)
    update(3, 3, 0)

    @pl.when(g == 0)
    def _():
        own_obs.wait()

    @pl.when(g != 0)
    def _():
        column_obs[0].wait_recv()

    mine_loc.wait()
    every_loc.wait_recv()
    mine_obs = local_copy(col_obs, all_obs.at[d], 3)
    every_obs = spread(col_obs, all_obs, 10, 5)
    pts[1] = points(all_loc[jnp.maximum(wi, 0)])
    pts[2] = points(all_loc[jnp.maximum(wj, 0)])
    covariance(1, 0)
    covariance(1, 1)
    lower(1, 0, inv)
    update(1, 1, 0)

    def one():
        covariance(2, 0)
        lower(2, 0, inv)

    def two():
        covariance(2, 1)
        update(2, 1, 0)

    def three():
        covariance(2, 2)
        update(2, 2, 0)

    def four():
        covariance(3, 1)
        update(3, 1, 0)

    def five():
        covariance(3, 2)
        update(3, 2, 0)

    inv1 = inverse(1, (one, two, three, four, five))
    lower(2, 1, inv1)
    update(2, 2, 1)

    def six():
        lower(3, 1, inv1)

    def seven():
        update(3, 2, 1)

    def eight():
        update(3, 3, 1)

    def nine():
        low[2, 0] = dot3(split(low[2, 1]), split(low[1, 0])) - low[2, 0]

    def ten():
        low[3, 0] = dot3(split(low[3, 1]), split(low[1, 0])) - low[3, 0]

    inv2 = inverse(2, (six, seven, eight, nine, ten))
    lower(3, 2, inv2)
    update(3, 3, 2)

    def eleven():
        put(2, -low[3, 2])

    def twelve():
        put(1, dot3(split(low[3, 2]), split(low[2, 1])) - low[3, 1])

    def thirteen():
        put(0, low[3, 0] - dot3(split(low[3, 2]), split(low[2, 0])))

    def dot_small(rows, mat, dims):
        high, rest = split(rows)
        return dot(high, mat[0], dims) + (dot(high, mat[1], dims) + dot(rest, mat[0], dims))

    def forward(own, before_rows, table):
        slots = jnp.concatenate(
            [before_rows, table[jnp.maximum(wi, 0)], table[jnp.maximum(wj, 0)]], axis=1
        )
        return own + dot_small(slots, g_mat, NT)

    def fourteen():
        pre[...] = forward(obs_v[...], prev_obs[...], all_obs)

    ahead_obs.wait()
    mine_obs.wait()
    every_obs.wait_recv()
    inv3 = inverse(3, (eleven, twelve, thirteen, fourteen))
    p_mat[0], p_mat[1] = split(inv3)

    def reduce(u, own, row, k, filler):
        hop[k] = u[:, :size]
        half = size // 2
        ui, uj = u[:, size : 2 * size], u[:, 2 * size :]

        def fill(m):
            fi = jnp.where(wi == m, 1.0, 0.0).astype(F32)
            fj = jnp.where(wj == m, 1.0, 0.0).astype(F32)
            block = fi * ui + fj * uj
            msg[k, m, :fields] = block[:, :half]
            msg[k, m, fields : 2 * fields] = block[:, half:]
            msg[k, m, 2 * fields :] = row

        returned = remote(hop.at[k], back.at[k], sem_s.at[11], sem_r.at[6 + k], before)
        targets = plane + [d]
        for m in targets[:LEAD]:
            fill(m)
        returned.start()
        for n, m in enumerate(plane):
            if n + LEAD < DEV:
                fill(targets[n + LEAD])
            remote(
                msg.at[k, m], rs.at[k, d], sem_s.at[12], sem_r.at[8 + k], {"grp": g, "dev": m}
            ).start()
        mine = local_copy(msg.at[k, d], rs.at[k, d], 0)
        filler()
        piece = rs.at[k, others]
        every = remote(piece, piece, sem_s.at[12], sem_r.at[8 + k], after)
        returned.wait()
        own = own + back[k]
        every.wait_recv()
        mine.wait()
        sums = [rs[k, n] for n in range(4)]
        for n in range(4, DEV):
            sums[n % 4] = sums[n % 4] + rs[k, n]
        total = (sums[0] + sums[1]) + (sums[2] + sums[3])
        held = first_group * jnp.concatenate(
            [own[:, :half], own[:, half:], jnp.zeros((1, half), F32)], axis=0
        )
        total = total + held
        xs[k, g] = total
        stage[k] = total
        copies = [
            remote(
                stage.at[k], xs.at[k, g], sem_s.at[12 + n], sem_r.at[9 + n + 3 * k],
                {"grp": lax.rem(g + n, GRP), "dev": d},
            )
            for n in (2, 1, 3)
        ]
        for c in copies:
            c.start()
        every.wait_send()
        for c in copies:
            c.wait()
        total = (xs[k, 0] + xs[k, 1]) + (xs[k, 2] + xs[k, 3])
        column = jnp.concatenate([total[:fields], total[fields : 2 * fields]], axis=1)
        image = jnp.where(g == 0, column, own)
        return image, column, total[2 * fields :]

    b, prec = obs_v[...], noise_v[...]
    v0 = pre[...]
    w0 = dot_small(v0, p_mat, NN)
    u0 = dot_small(w0, g_mat, NN)
    kept = prec * b

    def joined():
        left = (p_mat[0], p_mat[1])
        for k in range(3):
            cut = slice(k * size, (k + 1) * size)
            h_mat[0, :, cut], h_mat[1, :, cut] = split(
                dot3(left, (g_mat[0, :, cut], g_mat[1, :, cut]))
            )

    image0, column, row = reduce(u0, w0 + kept, to_row([b * b, v0 * w0 + kept * b]), 0, joined)
    rr0, p0 = from_row(row, 0, fields), from_row(row, 1, fields)
    alpha0 = rr0 / p0
    r1 = b - alpha0 * image0
    rcol[0] = r1
    rcol[1] = col_obs[...] - alpha0 * column
    ahead = remote(rcol.at[0], prev1, sem_s.at[11], sem_r.at[16], after)
    ahead.start()
    mine = local_copy(rcol.at[1], ag.at[d], 0)
    every = spread(rcol.at[1], ag, 12, 17)
    ahead.wait()
    mine.wait()
    every.wait()
    v1 = forward(r1, prev1[...], ag)
    w1 = dot_small(v1, p_mat, NN)
    u1 = dot_small(v1, h_mat, NN)
    kept = prec * r1
    image1, column, row = reduce(
        u1, w1 + kept, to_row([v1 * w1 + kept * r1, v1 * w0 + kept * b, r1 * r1]), 1,
        lambda: None,
    )
    s1, s2, rr1 = (from_row(row, k, fields) for k in range(3))
    beta = rr1 / rr0
    alpha1 = rr1 / (s1 + 2.0 * beta * s2 + beta * beta * p0)
    image1 = image1 + beta * image0
    out[0] = alpha0 * b + alpha1 * (r1 + beta * b)
    out[1] = r1 - alpha1 * image1
    every_loc.wait_send()
    every_obs.wait_send()

    @pl.when(g == 0)
    def _():
        for c in column_loc + column_obs:
            c.wait_send()


def local(locations, neighbours, observations, noise_prec):
    points, fields = locations.shape[2], observations.shape[1]
    vmem = pl.BlockSpec(memory_space=pltpu.VMEM)
    hbm = pl.BlockSpec(memory_space=pltpu.HBM)

    def f32(*shape):
        return pltpu.VMEM(shape, F32)

    tall = 2 * fields + 1
    held = [
        pltpu.with_memory_space_constraint(x, pltpu.HBM)
        for x in (neighbours, jnp.transpose(locations, (1, 0, 2)), observations, noise_prec)
    ]
    both = pl.pallas_call(
        kernel,
        out_shape=jax.ShapeDtypeStruct((2, fields, points), F32),
        in_specs=[hbm] * 4,
        out_specs=vmem,
        scratch_shapes=[
            pltpu.SMEM((1, neighbours.shape[1]), jnp.int32),
            f32(3, 1, points), f32(fields, points), f32(fields, points),
            f32(3, 1, points), f32(fields, points),
            f32(3, 1, points), f32(fields, points),
            f32(DEV, 3, 1, points), f32(DEV, fields, points),
            f32(4, 4, points, points), f32(4, 3, points, points),
            pltpu.VMEM((2, points, 3 * points), BF16), pltpu.VMEM((2, points, points), BF16),
            pltpu.VMEM((2, points, 3 * points), BF16), f32(fields, points),
            f32(2, DEV, tall, points // 2), f32(2, DEV, tall, points // 2),
            f32(2, GRP, tall, points // 2), f32(2, tall, points // 2),
            f32(2, fields, points), f32(2, fields, points),
            f32(2, fields, points), f32(fields, points), f32(DEV, fields, points),
            pltpu.SemaphoreType.DMA((4,)),
            pltpu.SemaphoreType.DMA((4,)),
            pltpu.SemaphoreType.DMA((16,)),
            pltpu.SemaphoreType.DMA((18,)),
        ],
        compiler_params=pltpu.CompilerParams(
            collective_id=0, has_side_effects=True, vmem_limit_bytes=48 << 20
        ),
    )(*held)
    return both[:1], both[1:]


def solution(mesh):
    placed = (
        P(("grp", "dev"), None, None),
        P(("grp", "dev"), None),
        P(("grp", "dev"), None, None),
        P(("grp", "dev"), None, None),
    )
    return jax.shard_map(
        local,
        mesh=mesh,
        in_specs=placed,
        out_specs=(P(("grp", "dev"), None, None), P(("grp", "dev"), None, None)),
        check_vma=False,
    )
```
